256 devices in a mesh: grp: 32 (over z_lo, x, core), slab: 8 (over z_hi, y).
Axes of the slice: x: 4, y: 4, z: 8 (z_hi: 2, z_lo: 4; z = z_hi * 4 + z_lo), core: 2. Of those that a mesh axis runs over, the one named last changes fastest.
Arguments:
- fwd_fields: float32 [32, 6, 64, 128, 128], P('grp', None, 'slab'), may hold values from -6 to 6
- adj_fields: float32 [32, 6, 64, 128, 128], P('grp', None, 'slab'), may hold values from -6 to 6
- density: float32 [64, 128, 128], P('slab', 'grp'), may hold values from 0 to 1
- block_ids: int32 [32], replicated, may hold values from 0 to 31, each once
- material_idx: int32 [32], replicated, may hold values from 0 to 3
- material_eps: float32 [4], replicated, may hold values from 1 to 12
- source_pos: int32 [32, 3], P('grp'), may hold values from 0 to 127, as said below
- wave_idx: int32 [32], P('grp'), may hold values from 0 to 3
Outputs:
- final_fields: float32 [32, 6, 64, 128, 128], P('grp', None, 'slab')
- grad_density: float32 [64, 128, 128], P('slab', 'grp')
The draws below stay inside these ranges and needn't reach their ends.
Inputs may be any that keep to these rules, and one draw needn't show every extreme that they name: `block_ids`: a permutation of the 32 blocks. `source_pos`: cells inside the window: z below 64, x below 128, y below 128; some group's z is 0, some group's x is 127 and some group's y is 127.
All inputs are finite; a program needn't handle non-finite values.
Results may differ from the reference program's by a relative error of at most 0.0003.
Values sent between devices are 32-bit elements; how exact they have to be, the bound alone decides.
A program may use at most 64 MiB of HBM per device.

```python
import math
import jax
import jax.numpy as jnp
from jax import lax

X = 128
Y = 128
STEPS = 4
NWAVE = 4
NMAT = 4
GROUPS = 32
NBLK = 32
BX = 4
NZ = 64


def draw_source_pos(key, part):
    key_z, key_x, key_y, key_pick = jax.random.split(key, 4)
    depth_pos = jax.random.randint(key_z, (GROUPS,), 0, NZ)
    row_pos = jax.random.randint(key_x, (GROUPS,), 0, X)
    col_pos = jax.random.randint(key_y, (GROUPS,), 0, Y)
    picks = jax.random.randint(key_pick, (3,), 0, GROUPS)
    group_ids = jnp.arange(GROUPS, dtype=jnp.int32)
    depth_pos = jnp.where(group_ids == picks[0], 0, depth_pos)
    row_pos = jnp.where(group_ids == picks[1], X - 1, row_pos)
    col_pos = jnp.where(group_ids == picks[2], Y - 1, col_pos)
    return jnp.stack([depth_pos, row_pos, col_pos], axis=1).astype(jnp.int32)


def with_ends(drawn, own_key, least, high):
    longest = drawn.shape.index(max(drawn.shape))
    spots = []
    for shift in (0, 1):
        where = [jax.random.randint(jax.random.fold_in(own_key, axis), (), 0, length) for axis, length in enumerate(drawn.shape)]
        where[longest] = (where[longest] + shift) % drawn.shape[longest]
        spots.append(tuple(where))
    return drawn.at[spots[0]].set(least).at[spots[1]].set(high)


def block_levels(rng, dims, pieces, smallest, top_value):
    loudness = 1.0
    for dim, shards_of in pieces:
        draws = jax.random.uniform(jax.random.fold_in(jax.random.fold_in(rng, 6), dim), (shards_of,), jnp.float32, smallest / len(pieces), top_value / len(pieces))
        loudness = loudness * jnp.repeat(jnp.exp(draws), dims[dim] // shards_of).reshape((-1,) + (1,) * (len(dims) - 1 - dim))
    return loudness


def bell_draw(key, extent, deviation, reach, cuts=(), kind=jnp.bfloat16):
    drawn = jax.random.normal(key, extent, jnp.float32) * deviation
    if len(cuts) > 0:
        drawn = block_levels(key, extent, cuts, -0.22, 0.18) * drawn
    return jnp.clip(drawn, min=-reach, max=reach).astype(kind)


def setup_inputs(seed: int = 0) -> dict:
    splits = jax.random.split(jax.random.key(seed), 9)
    fwd_fields = bell_draw(splits[0], (GROUPS, 6, NZ, X, Y), 1.0, 6.0, ((0, 32), (2, 8)), jnp.float32)
    adj_fields = bell_draw(splits[1], (GROUPS, 6, NZ, X, Y), 1.0, 6.0, ((0, 32), (2, 8)), jnp.float32)
    density = jnp.clip(1.0 * jax.random.uniform(splits[2], (NZ, X, Y), jnp.float32) ** block_levels(splits[2], (NZ, X, Y), ((0, 8), (1, 32)), -0.2, 0.2), 0.0, 1.0)
    block_ids = jax.random.permutation(splits[3], NBLK).astype(jnp.int32)
    material_idx = with_ends(jax.random.randint(splits[4], (NBLK,), 0, NMAT), jax.random.fold_in(splits[4], 1), 0, NMAT - 1).astype(jnp.int32)
    material_eps = jnp.clip(jnp.exp(jax.random.uniform(splits[5], (NMAT,), jnp.float32, math.log(1.0), math.log(12.0))), 1.0, 12.0)
    source_pos = draw_source_pos(jax.random.fold_in(splits[8], 71), 0)
    wave_idx = with_ends(jax.random.randint(splits[7], (GROUPS,), 0, NWAVE), jax.random.fold_in(splits[7], 1), 0, NWAVE - 1).astype(jnp.int32)
    return dict(fwd_fields=fwd_fields, adj_fields=adj_fields, density=density, block_ids=block_ids, material_idx=material_idx, material_eps=material_eps, source_pos=source_pos, wave_idx=wave_idx)


COURANT = 0.5
AMPLITUDE = 4.0

def fwd_diff(field, axis):
    pads = [(0, 0)] * field.ndim
    pads[axis] = (0, 1)
    padded = jnp.pad(field, pads)
    return lax.slice_in_dim(padded, 1, field.shape[axis] + 1, axis=axis) - field

def bwd_diff(field, axis):
    pads = [(0, 0)] * field.ndim
    pads[axis] = (1, 0)
    padded = jnp.pad(field, pads)
    return field - lax.slice_in_dim(padded, 0, field.shape[axis], axis=axis)

def filter_xy(values):
    padded = jnp.pad(values, ((0, 0), (1, 1), (1, 1)))
    rows = padded[:, :-2] + 2.0 * padded[:, 1:-1] + padded[:, 2:]
    return (rows[:, :, :-2] + 2.0 * rows[:, :, 1:-1] + rows[:, :, 2:]) / 16.0

def source_profile(zcoord, xcoord, ycoord, position, width_x, width_y):
    in_plane = (zcoord == position[0]).astype(jnp.float32)
    offset_x = (xcoord - position[1]).astype(jnp.float32) / (width_x / 4.0)
    offset_y = (ycoord - position[2]).astype(jnp.float32) / (width_y / 4.0)
    return in_plane * jnp.exp(-0.5 * (offset_x * offset_x + offset_y * offset_y))

def advance(comps, coef, drive):
    ex, ey, ez, hx, hy, hz = comps
    hx = hx - COURANT * (fwd_diff(ez, 2) - fwd_diff(ey, 0))
    hy = hy - COURANT * (fwd_diff(ex, 0) - fwd_diff(ez, 1))
    hz = hz - COURANT * (fwd_diff(ey, 1) - fwd_diff(ex, 2))
    ex = ex + coef * (bwd_diff(hz, 2) - bwd_diff(hy, 0))
    ey = ey + coef * (bwd_diff(hx, 0) - bwd_diff(hz, 1))
    ez = ez + coef * (bwd_diff(hy, 1) - bwd_diff(hx, 2)) + drive
    return (ex, ey, ez, hx, hy, hz)

def reference(fwd_fields, adj_fields, density, block_ids, material_idx, material_eps, source_pos, wave_idx):
    blocks = density.reshape(NZ, NBLK, BX, Y)
    placed = jnp.zeros_like(blocks).at[:, block_ids].set(blocks).reshape(NZ, X, Y)
    smooth = filter_xy(placed)
    base_rows = jnp.repeat(material_eps[material_idx], BX)
    eps = base_rows[None, :, None] + 3.0 * smooth
    coef = 0.5 / eps
    zcoord = lax.broadcasted_iota(jnp.int32, (NZ, X, Y), 0)
    xcoord = lax.broadcasted_iota(jnp.int32, (NZ, X, Y), 1)
    ycoord = lax.broadcasted_iota(jnp.int32, (NZ, X, Y), 2)

    def one_group(total, inputs):
        fwd, adj, pos, wave = inputs
        profile = source_profile(zcoord, xcoord, ycoord, pos, X, Y)
        omega = 2.0 * math.pi / (6.0 + 2.0 * wave.astype(jnp.float32))
        fcomp = tuple((fwd[c] for c in range(6)))
        acomp = tuple((adj[c] for c in range(6)))
        for step in range(STEPS):
            drive = AMPLITUDE * jnp.sin(omega * (step + 1.0)) * profile
            fcomp = advance(fcomp, coef, drive)
            acomp = advance(acomp, coef, 0.0)
            total = total + (fcomp[0] * acomp[0] + fcomp[1] * acomp[1] + fcomp[2] * acomp[2])
        return (total, jnp.stack(fcomp))
    total, finals = lax.scan(one_group, jnp.zeros((NZ, X, Y), jnp.float32), (fwd_fields, adj_fields, source_pos, wave_idx))
    scale = 3.0 / (STEPS * math.sqrt(GROUPS))
    grad = scale * filter_xy(total)
    grad_owner = grad.reshape(NZ, NBLK, BX, Y)[:, block_ids].reshape(NZ, X, Y)
    return (finals, grad_owner)
```

```python
import functools
import math

import jax
import jax.numpy as jnp
from jax import lax
from jax.experimental import pallas as pl
from jax.experimental.pallas import tpu as pltpu
from jax.sharding import PartitionSpec as P

STEPS = 4
COURANT = 0.5
AMPLITUDE = 4.0
MESH = pl.DeviceIdType.MESH
ROWS = 32
PAD = 8


def from_everyone(shard, axis):
    copies = jnp.broadcast_to(shard, (lax.axis_size(axis), *shard.shape))
    return lax.all_to_all(copies, axis, split_axis=0, concat_axis=0, tiled=True)


def sum_at_owner(shard, axis, dim):
    dims = shard.shape
    count = lax.axis_size(axis)
    pieces = shard.reshape(*dims[:dim], count, dims[dim] // count, *dims[dim + 1 :])
    pieces = jnp.moveaxis(pieces, dim, 0)
    arrived = lax.all_to_all(pieces, axis, split_axis=0, concat_axis=0, tiled=True)
    return arrived.sum(axis=0)


def filter_xy(values):
    padded = jnp.pad(values, ((0, 0), (1, 1), (1, 1)))
    rows = padded[:, :-2] + 2.0 * padded[:, 1:-1] + padded[:, 2:]
    return (rows[:, :, :-2] + 2.0 * rows[:, :, 1:-1] + rows[:, :, 2:]) / 16.0


def evolve_kernel(
    pos_ref, wave_ref, fwd_ref, adj_ref, coef_ref, out_ref, tot_ref,
    st, el, eu, ha, ha0, sup, sdn, drv, load_sem, store_sem, up_s, up_r, h_s, h_r, dn_s, dn_r,
):
    depth, width_x, width_y = coef_ref.shape
    top = depth - 1
    grp, slab = lax.axis_index("grp"), lax.axis_index("slab")
    slabs = lax.axis_size("slab")
    has_up, has_dn = slab < slabs - 1, slab > 0
    inner = pl.ds(PAD, width_x)
    fields = (fwd_ref, adj_ref)

    def up_copy(ev, n, src):
        return pltpu.make_async_remote_copy(
            src_ref=src, dst_ref=el.at[ev, n, :, pl.ds(0, width_x), :], send_sem=up_s.at[ev, n], recv_sem=up_r.at[ev, n],
            device_id=(grp, slab + 1), device_id_type=MESH)

    def h_copy(ev):
        return pltpu.make_async_remote_copy(
            src_ref=fields[ev].at[0, 3:5, top], dst_ref=ha0.at[ev], send_sem=h_s.at[ev], recv_sem=h_r.at[ev],
            device_id=(grp, slab + 1), device_id_type=MESH)

    def dn_copy(ev, n, src):
        return pltpu.make_async_remote_copy(
            src_ref=src, dst_ref=eu.at[ev, n], send_sem=dn_s.at[ev, n], recv_sem=dn_r.at[ev, n],
            device_id=(grp, slab - 1), device_id_type=MESH)

    barrier = pltpu.get_barrier_semaphore()

    @pl.when(has_up)
    def _():
        pl.semaphore_signal(barrier, inc=1, device_id=(grp, slab + 1), device_id_type=MESH)

    @pl.when(has_dn)
    def _():
        pl.semaphore_signal(barrier, inc=1, device_id=(grp, slab - 1), device_id_type=MESH)

    loads = [
        pltpu.make_async_copy(fields[ev].at[0], st.at[ev, :, :, inner, :], load_sem.at[ev]) for ev in range(2)
    ]
    for copy in loads:
        copy.start()

    zeros = jnp.zeros((PAD, width_y), jnp.float32)

    @pl.loop(0, depth)
    def _(z):
        for ev in range(2):
            for c in (1, 2):
                st[ev, c, z, PAD + width_x :, :] = zeros
            for c in (4, 5):
                st[ev, c, z, :PAD, :] = zeros

    for ev in range(2):
        for n in range(STEPS):
            el[ev, n, 2, width_x:, :] = zeros
    row = lax.broadcasted_iota(jnp.int32, (width_x, width_y), 0)
    col = lax.broadcasted_iota(jnp.int32, (width_x, width_y), 1)
    dx = (row - pos_ref[0, 1]).astype(jnp.float32) / (width_x / 4.0)
    dy = (col - pos_ref[0, 2]).astype(jnp.float32) / (width_y / 4.0)
    profile = jnp.exp(-0.5 * (dx * dx + dy * dy))
    wave = jnp.full((8, width_y), wave_ref[0], jnp.int32).astype(jnp.float32)
    omega = 2.0 * math.pi / (6.0 + 2.0 * wave)
    for n in range(STEPS):
        drv[n] = (AMPLITUDE * jnp.sin(omega * (n + 1.0)))[:1] * profile
    lane = lax.broadcasted_iota(jnp.int32, (ROWS, width_y), 1)
    is_first, is_last = lane == 0, lane == width_y - 1

    @pl.when(jnp.logical_not(has_up))
    def _():
        eu[...] = jnp.zeros_like(eu)

    @pl.when(jnp.logical_not(has_dn))
    def _():
        ha[...] = jnp.zeros_like(ha)

    pl.semaphore_wait(barrier, has_up.astype(jnp.int32) + has_dn.astype(jnp.int32))
    for ev in range(2):

        @pl.when(has_up)
        def _():
            up_copy(ev, 0, fields[ev].at[0, 0:3, top]).start()
            h_copy(ev).start()

        @pl.when(has_dn)
        def _():
            dn_copy(ev, 0, fields[ev].at[0, 0:2, 0]).start()

    def next_y(v):
        return jnp.where(is_last, 0.0, pltpu.roll(v, width_y - 1, axis=1))

    def prev_y(v):
        return jnp.where(is_first, 0.0, pltpu.roll(v, 1, axis=1))

    def chunks():
        return [(r, pl.ds(PAD + r, ROWS)) for r in range(0, width_x, ROWS)]

    def h_layer(ev, z, above):
        for r, here in chunks():
            ahead = pl.ds(PAD + r + 1, ROWS)
            ex, ey, ez = (st[ev, c, z, here, :] for c in range(3))
            exu, eyu = above(r)
            dyz = next_y(ez) - ez
            dyx = next_y(ex) - ex
            st[ev, 3, z, here, :] += -COURANT * (dyz - (eyu - ey))
            st[ev, 4, z, here, :] += -COURANT * ((exu - ex) - (st[ev, 2, z, ahead, :] - ez))
            st[ev, 5, z, here, :] += -COURANT * ((st[ev, 1, z, ahead, :] - ey) - dyx)

    def e_layer(ev, n, z, below, send=None):
        plane = jnp.where((slab * depth + z == pos_ref[0, 0]) & (ev == 0), 1.0, 0.0)
        for r, here in chunks():
            back = pl.ds(PAD + r - 1, ROWS)
            out = pl.ds(r, ROWS)
            hx, hy, hz = (st[ev, c, z, here, :] for c in range(3, 6))
            hxd, hyd = below(r)
            coef = coef_ref[z, out, :]
            ex = st[ev, 0, z, here, :] + coef * ((hz - prev_y(hz)) - (hy - hyd))
            ey = st[ev, 1, z, here, :] + coef * ((hx - hxd) - (hz - st[ev, 5, z, back, :]))
            ez = st[ev, 2, z, here, :] + coef * ((hy - st[ev, 4, z, back, :]) - (hx - prev_y(hx)))
            ez = ez + plane * drv[n, out, :]
            for c, v in enumerate((ex, ey, ez)):
                st[ev, c, z, here, :] = v
            if send is not None:
                for c in range(send.shape[0]):
                    send[c, out, :] = (ex, ey, ez)[c]

    @pl.loop(0, 2 * STEPS)
    def _(i):
        n, ev = i // 2, lax.rem(i, 2)

        @pl.when(n == 0)
        def _():
            pltpu.make_async_copy(fwd_ref.at[0], st.at[ev, :, :, inner, :], load_sem.at[ev]).wait()

        @pl.loop(0, top)
        def _(z):
            h_layer(ev, z, lambda r: (st[ev, 0, z + 1, pl.ds(PAD + r, ROWS), :], st[ev, 1, z + 1, pl.ds(PAD + r, ROWS), :]))

        def below(z):
            return lambda r: (st[ev, 3, z - 1, pl.ds(PAD + r, ROWS), :], st[ev, 4, z - 1, pl.ds(PAD + r, ROWS), :])

        @pl.loop(1, top)
        def _(z):
            e_layer(ev, n, z, below(z))

        @pl.when(has_up)
        def _():
            dn_copy(ev, n, sdn.at[ev, n]).wait_recv()

        h_layer(ev, top, lambda r: (eu[ev, n, 0, pl.ds(r, ROWS), :], eu[ev, n, 1, pl.ds(r, ROWS), :]))
        e_layer(ev, n, top, below(top), sup.at[ev, n])

        @pl.when(has_up & (n < STEPS - 1))
        def _():
            up_copy(ev, n + 1, sup.at[ev, n]).start()

        @pl.when(has_dn)
        def _():
            up_copy(ev, n, sup.at[ev, n]).wait_recv()

            @pl.when(n == 0)
            def _():
                pltpu.make_async_remote_copy(
                    src_ref=fwd_ref.at[0, 3:5, top], dst_ref=ha0.at[ev], send_sem=h_s.at[ev], recv_sem=h_r.at[ev],
                    device_id=(grp, slab - 1), device_id_type=MESH).wait_recv()
                ha[ev] = ha0[ev]

            for r, here in chunks():
                out, ahead = pl.ds(r, ROWS), pl.ds(r + 1, ROWS)
                ex, ey, ez = (el[ev, n, c, out, :] for c in range(3))
                ha[ev, 0, out, :] += -COURANT * ((next_y(ez) - ez) - (st[ev, 1, 0, here, :] - ey))
                ha[ev, 1, out, :] += -COURANT * ((st[ev, 0, 0, here, :] - ex) - (el[ev, n, 2, ahead, :] - ez))

        e_layer(ev, n, 0, lambda r: (ha[ev, 0, pl.ds(r, ROWS), :], ha[ev, 1, pl.ds(r, ROWS), :]), sdn.at[ev, n])

        @pl.when(has_dn & (n < STEPS - 1))
        def _():
            dn_copy(ev, n + 1, sdn.at[ev, n]).start()

        @pl.when(i == 2 * STEPS - 2)
        def _():
            pltpu.make_async_copy(st.at[0, :, :, inner, :], out_ref.at[0], store_sem).start()

        @pl.when(ev == 1)
        def _():
            @pl.loop(0, depth)
            def _(z):
                for r, here in chunks():
                    out = pl.ds(r, ROWS)
                    new = sum(st[0, c, z, here, :] * st[1, c, z, here, :] for c in range(3))
                    old = jnp.where(n == 0, 0.0, tot_ref[z, out, :])
                    tot_ref[z, out, :] = old + new

    pltpu.make_async_copy(st.at[0, :, :, inner, :], out_ref.at[0], store_sem).wait()
    for ev in range(2):

        @pl.when(has_up)
        def _():
            up_copy(ev, 0, fields[ev].at[0, 0:3, top]).wait_send()
            h_copy(ev).wait_send()
            for n in range(1, STEPS):
                up_copy(ev, n, sup.at[ev, n - 1]).wait_send()

        @pl.when(has_dn)
        def _():
            dn_copy(ev, 0, fields[ev].at[0, 0:2, 0]).wait_send()
            for n in range(1, STEPS):
                dn_copy(ev, n, sdn.at[ev, n - 1]).wait_send()


def evolve(fwd_fields, adj_fields, coef, source_pos, wave_idx):
    depth, width_x, width_y = coef.shape
    f32 = jnp.float32
    layer = (width_x, width_y)
    smem = pl.BlockSpec(memory_space=pltpu.SMEM)
    vmem = pl.BlockSpec(memory_space=pltpu.VMEM)
    hbm = pl.BlockSpec(memory_space=pl.ANY)
    dma = pltpu.SemaphoreType.DMA
    return pl.pallas_call(
        evolve_kernel,
        out_shape=(
            jax.ShapeDtypeStruct(fwd_fields.shape, f32),
            jax.ShapeDtypeStruct(coef.shape, f32),
        ),
        in_specs=[smem, smem, hbm, hbm, vmem],
        out_specs=(hbm, vmem),
        scratch_shapes=[
            pltpu.VMEM((2, 6, depth, width_x + 2 * PAD, width_y), f32),
            pltpu.VMEM((2, STEPS, 3, width_x + PAD, width_y), f32),
            pltpu.VMEM((2, STEPS, 2, *layer), f32),
            pltpu.VMEM((2, 2, *layer), f32),
            pltpu.VMEM((2, 2, *layer), f32),
            pltpu.VMEM((2, STEPS, 3, *layer), f32),
            pltpu.VMEM((2, STEPS, 2, *layer), f32),
            pltpu.VMEM((STEPS, *layer), f32),
            dma((2,)), dma(()), dma((2, STEPS)), dma((2, STEPS)), dma((2,)), dma((2,)), dma((2, STEPS)), dma((2, STEPS)),
        ],
        compiler_params=pltpu.CompilerParams(collective_id=0, has_side_effects=True, vmem_limit_bytes=40 << 20),
        name="evolve",
    )(source_pos, wave_idx, fwd_fields, adj_fields, coef)


def per_device(
    fwd_fields, adj_fields, density, block_ids, material_idx, material_eps, source_pos, wave_idx
):
    depth, width_x, width_y = fwd_fields.shape[2:]
    nblock = block_ids.shape[0]
    block_rows = width_x // nblock
    pieces = from_everyone(density, "grp")
    blocks = jnp.moveaxis(pieces, 0, 1)
    placed = jnp.zeros_like(blocks).at[:, block_ids].set(blocks).reshape(depth, width_x, width_y)
    smooth = filter_xy(placed)
    onehot = (
        material_idx[:, None] == jnp.arange(material_eps.shape[0], dtype=jnp.int32)[None, :]
    ).astype(jnp.float32)
    base = jnp.sum(onehot * material_eps[None, :], axis=1)
    base_rows = jnp.repeat(base, block_rows)
    eps = base_rows[None, :, None] + 3.0 * smooth
    coef = 0.5 / eps
    finals, total = evolve(fwd_fields, adj_fields, coef, source_pos, wave_idx)
    grad_sum = sum_at_owner(
        filter_xy(total)
        .reshape(depth, nblock, block_rows, width_y)[:, block_ids]
        .reshape(depth, width_x, width_y),
        "grp",
        1,
    )
    scale = 3.0 / (STEPS * math.sqrt(lax.axis_size("grp")))
    return (finals, grad_sum * scale)


def solution(mesh):
    placed = (
        P("grp", None, "slab", None, None),
        P("grp", None, "slab", None, None),
        P("slab", "grp", None),
        P(),
        P(),
        P(),
        P("grp", None),
        P("grp"),
    )
    return jax.shard_map(
        per_device,
        mesh=mesh,
        in_specs=placed,
        out_specs=(P("grp", None, "slab", None, None), P("slab", "grp", None)),
        check_vma=False,
    )
```

```python
import math

import jax
import jax.numpy as jnp
from jax import lax
from jax.experimental import pallas as pl
from jax.experimental.pallas import tpu as pltpu
from jax.sharding import PartitionSpec as P

STEPS = 4
COURANT = 0.5
AMPLITUDE = 4.0
MESH = pl.DeviceIdType.MESH
ROWS = 32
PAD = 8
GROUPS = 32
RUNS = 4
OWN = 32
INNER = 24
HIGHEST = lax.Precision.HIGHEST


def evolve_kernel(
    pos_ref, wave_ref, ids_ref, mat_ref, eps_ref, dens_ref, fwd_ref, adj_ref, out_ref, grad_ref,
    st, coef_ref, tot_ref, el, eu, ha, ha0, sup, sdn, drv, rel, relh, gath, sendb, recvb, wmat, wtr, base,
    load_sem, store_sem, u1_s, u1_r, u2_s, u2_r, h1_s, h1_r, h2_s, h2_r, d1_s, d1_r, d2_s, d2_r,
    rl_s, rl_r, rh_s, rh_r, ga_s, ga_r, ri_s, ri_r, rb_s, rb_r,
):
    depth, width_x, width_y = coef_ref.shape
    top = depth - 1
    grp, slab = lax.axis_index("grp"), lax.axis_index("slab")
    slabs = lax.axis_size("slab")
    last = slabs - 1
    low, high = slabs // 2 - 1, slabs // 2
    has_up, has_dn = slab < last, slab > 0
    run = grp // (GROUPS // RUNS)
    mid = (run == 1) | (run == 2)
    mid_low, mid_high = mid & (slab == low), mid & (slab == high)
    relay_up, relay_dn = mid & (slab == 0), mid & (slab == last)
    inner = pl.ds(PAD, width_x)
    whole = pl.ds(0, width_x)
    fields = (fwd_ref, adj_ref)

    def copy_to(src, dst, send, recv, to_slab):
        return pltpu.make_async_remote_copy(
            src_ref=src, dst_ref=dst, send_sem=send, recv_sem=recv, device_id=(grp, to_slab), device_id_type=MESH)

    def u1(ev, n, src):
        return copy_to(src, el.at[ev, n, 0:2, whole, :], u1_s.at[ev, n], u1_r.at[ev, n], slab + 1)

    def u2(ev, n, src):
        return copy_to(src, el.at[ev, n, 2, whole, :], u2_s.at[ev, n], u2_r.at[ev, n], slab + 1)

    def u2_via(ev, n, src):
        return copy_to(src, rel.at[ev, n], u2_s.at[ev, n], rl_r.at[ev, n], 0)

    def h1(ev, src):
        return copy_to(src, ha0.at[ev, 1], h1_s.at[ev], h1_r.at[ev], slab + 1)

    def h2(ev, src):
        return copy_to(src, ha0.at[ev, 0], h2_s.at[ev], h2_r.at[ev], slab + 1)

    def h2_via(ev, src):
        return copy_to(src, relh.at[ev], h2_s.at[ev], rh_r.at[ev], 0)

    def d1(ev, n, src):
        return copy_to(src, eu.at[ev, n, 0], d1_s.at[ev, n], d1_r.at[ev, n], slab - 1)

    def d2(ev, n, src):
        return copy_to(src, eu.at[ev, n, 1], d2_s.at[ev, n], d2_r.at[ev, n], slab - 1)

    def d2_via(ev, n, src):
        return copy_to(src, rel.at[ev, n], d2_s.at[ev, n], rl_r.at[ev, n], last)

    def relay_e_up(ev, n):
        return copy_to(rel.at[ev, n], el.at[ev, n, 2, whole, :], rl_s.at[ev, n], u2_r.at[ev, n], high)

    def relay_h_up(ev):
        return copy_to(relh.at[ev], ha0.at[ev, 0], rh_s.at[ev], h2_r.at[ev], high)

    def relay_e_dn(ev, n):
        return copy_to(rel.at[ev, n], eu.at[ev, n, 1], rl_s.at[ev, n], d2_r.at[ev, n], low)

    def peer_copy(src, dst, send, recv, peer):
        return pltpu.make_async_remote_copy(
            src_ref=src, dst_ref=dst, send_sem=send, recv_sem=recv, device_id=(peer, slab), device_id_type=MESH)

    def peer_of(d):
        return lax.rem(grp + d, GROUPS)

    def own_rows(k, first, count):
        return pl.ds(pl.multiple_of(k * OWN + first, 8), count)

    def gather_copy(d):
        return peer_copy(dens_ref, gath.at[own_rows(grp, 0, OWN), :], ga_s.at[d], ga_r.at[grp], peer_of(d))

    def sums_copy(d, first, count, send, recv):
        return peer_copy(sendb.at[own_rows(peer_of(d), first, count), :], recvb.at[own_rows(grp, first, count), :],
                         send.at[d], recv.at[grp], peer_of(d))

    barrier = pltpu.get_barrier_semaphore()

    @pl.loop(1, GROUPS)
    def _(d):
        pl.semaphore_signal(barrier, inc=1, device_id=(peer_of(d), slab), device_id_type=MESH)

    def greet(cond, to_slab):
        @pl.when(cond)
        def _():
            pl.semaphore_signal(barrier, inc=1, device_id=(grp, to_slab), device_id_type=MESH)

    greet(has_up, slab + 1)
    greet(has_dn, slab - 1)
    greet(mid_low | mid_high, 0)
    greet(mid_low | mid_high, last)
    greet(relay_up | relay_dn, low)
    greet(relay_up | relay_dn, high)

    for ev in range(2):
        pltpu.make_async_copy(fields[ev].at[0], st.at[ev, :, :, inner, :], load_sem.at[ev]).start()

    zeros = jnp.zeros((PAD, width_y), jnp.float32)

    @pl.loop(0, depth)
    def _(z):
        for ev in range(2):
            for c in (1, 2):
                st[ev, c, z, PAD + width_x :, :] = zeros
            for c in (4, 5):
                st[ev, c, z, :PAD, :] = zeros

    for ev in range(2):
        for n in range(STEPS):
            el[ev, n, 2, width_x:, :] = zeros
    row = lax.broadcasted_iota(jnp.int32, (width_x, width_y), 0)
    col = lax.broadcasted_iota(jnp.int32, (width_x, width_y), 1)
    dx = (row - pos_ref[0, 1]).astype(jnp.float32) / (width_x / 4.0)
    dy = (col - pos_ref[0, 2]).astype(jnp.float32) / (width_y / 4.0)
    profile = jnp.exp(-0.5 * (dx * dx + dy * dy))
    wave = jnp.full((8, width_y), wave_ref[0], jnp.int32).astype(jnp.float32)
    omega = 2.0 * math.pi / (6.0 + 2.0 * wave)
    for n in range(STEPS):
        drv[n] = (AMPLITUDE * jnp.sin(omega * (n + 1.0)))[:1] * profile

    blocks = ids_ref.shape[0]
    block_rows = width_x // blocks
    slot = lax.rem(col, blocks)
    target = col // blocks
    for k in range(blocks):
        target = target + jnp.where(slot == k, ids_ref[k] * block_rows, 0)
    apart = jnp.abs(row - target)
    weights = jnp.where(apart == 0, 0.5, jnp.where(apart == 1, 0.25, 0.0))
    wmat[...] = weights
    wtr[...] = weights.T
    part = lax.broadcasted_iota(jnp.int32, (8, width_y), 0) // block_rows
    per_tile = 8 // block_rows
    for tile in range(width_x // 8):
        value = jnp.zeros((8, width_y), jnp.float32)
        for q in range(per_tile):
            value = jnp.where(part == q, eps_ref[mat_ref[tile * per_tile + q]], value)
        base[8 * tile : 8 * tile + 8, :] = value
    lane = lax.broadcasted_iota(jnp.int32, (ROWS, width_y), 1)
    is_first, is_last = lane == 0, lane == width_y - 1

    @pl.when(jnp.logical_not(has_up))
    def _():
        eu[...] = jnp.zeros_like(eu)

    @pl.when(jnp.logical_not(has_dn))
    def _():
        ha[...] = jnp.zeros_like(ha)

    own = pl.ds(pl.multiple_of(grp * OWN, 8), OWN)
    gath[own, :] = dens_ref[...]
    extra = jnp.where(mid_low | mid_high | relay_up | relay_dn, 2, 0)
    pl.semaphore_wait(barrier, GROUPS - 1 + has_up.astype(jnp.int32) + has_dn.astype(jnp.int32) + extra)

    def send_first(ev):
        f = fields[ev]

        @pl.when(has_dn)
        def _():
            d1(ev, 0, f.at[0, 0, 0]).start()

            @pl.when(mid_high)
            def _():
                d2_via(ev, 0, f.at[0, 1, 0]).start()

            @pl.when(jnp.logical_not(mid_high))
            def _():
                d2(ev, 0, f.at[0, 1, 0]).start()

        @pl.when(has_up)
        def _():
            @pl.when(mid_low)
            def _():
                u2_via(ev, 0, f.at[0, 2, top]).start()
                h2_via(ev, f.at[0, 3, top]).start()

            @pl.when(jnp.logical_not(mid_low))
            def _():
                u2(ev, 0, f.at[0, 2, top]).start()
                h2(ev, f.at[0, 3, top]).start()

            u1(ev, 0, f.at[0, 0:2, top]).start()
            h1(ev, f.at[0, 4, top]).start()

    send_first(0)

    @pl.loop(1, GROUPS)
    def _(d):
        gather_copy(d).start()

    send_first(1)

    def next_y(v):
        return jnp.where(is_last, 0.0, pltpu.roll(v, width_y - 1, axis=1))

    def prev_y(v):
        return jnp.where(is_first, 0.0, pltpu.roll(v, 1, axis=1))

    def chunks():
        return [(r, pl.ds(PAD + r, ROWS)) for r in range(0, width_x, ROWS)]

    def h_layer(ev, z, above):
        for r, here in chunks():
            ahead = pl.ds(PAD + r + 1, ROWS)
            ex, ey, ez = (st[ev, c, z, here, :] for c in range(3))
            exu, eyu = above(r)
            dyz = next_y(ez) - ez
            dyx = next_y(ex) - ex
            st[ev, 3, z, here, :] += -COURANT * (dyz - (eyu - ey))
            st[ev, 4, z, here, :] += -COURANT * ((exu - ex) - (st[ev, 2, z, ahead, :] - ez))
            st[ev, 5, z, here, :] += -COURANT * ((st[ev, 1, z, ahead, :] - ey) - dyx)

    def e_layer(ev, n, z, below, send=None):
        plane = jnp.where((slab * depth + z == pos_ref[0, 0]) & (ev == 0), 1.0, 0.0)
        for r, here in chunks():
            back = pl.ds(PAD + r - 1, ROWS)
            out = pl.ds(r, ROWS)
            hx, hy, hz = (st[ev, c, z, here, :] for c in range(3, 6))
            hxd, hyd = below(r)
            coef = coef_ref[z, out, :]
            ex = st[ev, 0, z, here, :] + coef * ((hz - prev_y(hz)) - (hy - hyd))
            ey = st[ev, 1, z, here, :] + coef * ((hx - hxd) - (hz - st[ev, 5, z, back, :]))
            ez = st[ev, 2, z, here, :] + coef * ((hy - st[ev, 4, z, back, :]) - (hx - prev_y(hx)))
            ez = ez + plane * drv[n, out, :]
            for c, v in enumerate((ex, ey, ez)):
                st[ev, c, z, here, :] = v
            if send is not None:
                for c in range(send.shape[0]):
                    send[c, out, :] = (ex, ey, ez)[c]

    def filter_y(v):
        left = jnp.where(col == 0, 0.0, pltpu.roll(v, 1, axis=1))
        right = jnp.where(col == width_y - 1, 0.0, pltpu.roll(v, width_y - 1, axis=1))
        return (left + 2.0 * v + right) * 0.25

    def h_inside(ev, z):
        h_layer(ev, z, lambda r: (st[ev, 0, z + 1, pl.ds(PAD + r, ROWS), :], st[ev, 1, z + 1, pl.ds(PAD + r, ROWS), :]))

    def below(ev, z):
        return lambda r: (st[ev, 3, z - 1, pl.ds(PAD + r, ROWS), :], st[ev, 4, z - 1, pl.ds(PAD + r, ROWS), :])

    def add_total(n, z):
        for r, here in chunks():
            out = pl.ds(r, ROWS)
            new = sum(st[0, c, z, here, :] * st[1, c, z, here, :] for c in range(3))
            tot_ref[z, out, :] = jnp.where(n == 0, 0.0, tot_ref[z, out, :]) + new

    def make_coef():
        @pl.loop(1, GROUPS)
        def _(d):
            src = peer_of(d)
            peer_copy(dens_ref, gath.at[own_rows(src, 0, OWN), :], ga_s.at[d], ga_r.at[src], src).wait_recv()

        @pl.loop(0, depth)
        def _(z):
            rows = jnp.concatenate(
                [gath[pl.ds(z * block_rows + j, blocks, stride=OWN), :] for j in range(block_rows)], axis=0
            )
            smooth = jnp.dot(wmat[...], filter_y(rows), precision=HIGHEST, preferred_element_type=jnp.float32)
            coef_ref[z] = 0.5 / (base[...] + 3.0 * smooth)

    scale = 3.0 / (STEPS * math.sqrt(GROUPS))

    def pack_sums(z, place):
        back = jnp.dot(wtr[...], filter_y(tot_ref[z]), precision=HIGHEST, preferred_element_type=jnp.float32) * scale
        for j in range(block_rows):
            sendb[pl.ds(place * block_rows + j, blocks, stride=OWN), :] = back[j * blocks : (j + 1) * blocks]

    def forward(ev, n):
        @pl.when(relay_up)
        def _():
            u2_via(ev, n, rel.at[ev, n]).wait_recv()
            relay_e_up(ev, n).start()

            @pl.when(n == 0)
            def _():
                h2_via(ev, relh.at[ev]).wait_recv()
                relay_h_up(ev).start()

        @pl.when(relay_dn)
        def _():
            d2_via(ev, n, rel.at[ev, n]).wait_recv()
            relay_e_dn(ev, n).start()

    def edges(ev, n, sending):
        @pl.when(has_up)
        def _():
            d1(ev, n, sdn.at[ev, n, 0]).wait_recv()
            d2(ev, n, sdn.at[ev, n, 1]).wait_recv()

        h_layer(ev, top, lambda r: (eu[ev, n, 0, pl.ds(r, ROWS), :], eu[ev, n, 1, pl.ds(r, ROWS), :]))
        e_layer(ev, n, top, below(ev, top), sup.at[ev, n])
        if sending:

            @pl.when(has_up)
            def _():
                @pl.when(mid_low)
                def _():
                    u2_via(ev, n + 1, sup.at[ev, n, 2]).start()

                @pl.when(jnp.logical_not(mid_low))
                def _():
                    u2(ev, n + 1, sup.at[ev, n, 2]).start()

                u1(ev, n + 1, sup.at[ev, n, 0:2]).start()

        @pl.when(has_dn)
        def _():
            u1(ev, n, sup.at[ev, n, 0:2]).wait_recv()
            u2(ev, n, sup.at[ev, n, 2]).wait_recv()

            @pl.when(n == 0)
            def _():
                h1(ev, ha0.at[ev, 1]).wait_recv()
                h2(ev, ha0.at[ev, 0]).wait_recv()
                ha[ev] = ha0[ev]

            for r, here in chunks():
                out, ahead = pl.ds(r, ROWS), pl.ds(r + 1, ROWS)
                ex, ey, ez = (el[ev, n, c, out, :] for c in range(3))
                ha[ev, 0, out, :] += -COURANT * ((next_y(ez) - ez) - (st[ev, 1, 0, here, :] - ey))
                ha[ev, 1, out, :] += -COURANT * ((st[ev, 0, 0, here, :] - ex) - (el[ev, n, 2, ahead, :] - ez))

        e_layer(ev, n, 0, lambda r: (ha[ev, 0, pl.ds(r, ROWS), :], ha[ev, 1, pl.ds(r, ROWS), :]), sdn.at[ev, n])
        if sending:

            @pl.when(has_dn)
            def _():
                d1(ev, n + 1, sdn.at[ev, n, 0]).start()

                @pl.when(mid_high)
                def _():
                    d2_via(ev, n + 1, sdn.at[ev, n, 1]).start()

                @pl.when(jnp.logical_not(mid_high))
                def _():
                    d2(ev, n + 1, sdn.at[ev, n, 1]).start()

        forward(ev, n)

    @pl.loop(0, 2 * STEPS)
    def _(i):
        n, ev = i // 2, lax.rem(i, 2)

        @pl.when(n == 0)
        def _():
            pltpu.make_async_copy(fwd_ref.at[0], st.at[ev, :, :, inner, :], load_sem.at[ev]).wait()

        h_inside(ev, 0)
        h_inside(ev, top - 1)

        @pl.when(i == 0)
        def _():
            make_coef()

        @pl.when(n < STEPS - 1)
        def _():
            edges(ev, n, True)

        @pl.loop(1, top - 1)
        def _(z):
            h_inside(ev, z)

        @pl.loop(1, top)
        def _(z):
            e_layer(ev, n, z, below(ev, z))

        @pl.when(ev == 1)
        def _():
            @pl.loop(1, top)
            def _(z):
                add_total(n, z)

        @pl.when(i == 2 * STEPS - 1)
        def _():
            @pl.loop(1, top)
            def _(z):
                pack_sums(z, z - 1)

            @pl.loop(1, GROUPS)
            def _(d):
                sums_copy(d, 0, INNER, ri_s, ri_r).start()

        @pl.when(n == STEPS - 1)
        def _():
            edges(ev, n, False)

        @pl.when(ev == 1)
        def _():
            add_total(n, 0)
            add_total(n, top)

        @pl.when(i == 2 * STEPS - 2)
        def _():
            pltpu.make_async_copy(st.at[0, :, :, inner, :], out_ref.at[0], store_sem).start()

    pack_sums(0, top - 1)
    pack_sums(top, top)

    @pl.loop(1, GROUPS)
    def _(d):
        sums_copy(d, INNER, OWN - INNER, rb_s, rb_r).start()

    def arrived(first, count, send, recv):
        def add(d, acc):
            src = peer_of(d)
            rows = own_rows(src, first, count)
            peer_copy(sendb.at[rows, :], recvb.at[rows, :], send.at[d], recv.at[src], src).wait_recv()
            return acc + recvb[rows, :]

        return lax.fori_loop(1, GROUPS, add, sendb[own_rows(grp, first, count), :])

    middle = arrived(0, INNER, ri_s, ri_r)
    for z in range(1, top):
        grad_ref[z * block_rows : (z + 1) * block_rows, :] = middle[(z - 1) * block_rows : z * block_rows]
    ends = arrived(INNER, OWN - INNER, rb_s, rb_r)
    grad_ref[0:block_rows, :] = ends[:block_rows]
    grad_ref[top * block_rows : depth * block_rows, :] = ends[block_rows:]

    pltpu.make_async_copy(st.at[0, :, :, inner, :], out_ref.at[0], store_sem).wait()

    @pl.loop(1, GROUPS)
    def _(d):
        gather_copy(d).wait_send()
        sums_copy(d, 0, INNER, ri_s, ri_r).wait_send()
        sums_copy(d, INNER, OWN - INNER, rb_s, rb_r).wait_send()

    @pl.loop(0, 2)
    def _(ev):
        @pl.when(has_up)
        def _():
            h1(ev, ha0.at[ev, 1]).wait_send()
            h2(ev, ha0.at[ev, 0]).wait_send()

        @pl.when(relay_up)
        def _():
            relay_h_up(ev).wait_send()

        @pl.loop(0, STEPS)
        def _(n):
            @pl.when(has_up)
            def _():
                u1(ev, n, sup.at[ev, n, 0:2]).wait_send()
                u2(ev, n, sup.at[ev, n, 2]).wait_send()

            @pl.when(has_dn)
            def _():
                d1(ev, n, sdn.at[ev, n, 0]).wait_send()
                d2(ev, n, sdn.at[ev, n, 1]).wait_send()

            @pl.when(relay_up)
            def _():
                relay_e_up(ev, n).wait_send()

            @pl.when(relay_dn)
            def _():
                relay_e_dn(ev, n).wait_send()


def per_device(
    fwd_fields, adj_fields, density, block_ids, material_idx, material_eps, source_pos, wave_idx
):
    depth, width_x, width_y = fwd_fields.shape[2:]
    f32 = jnp.float32
    layer = (width_x, width_y)
    rows = density.shape[0] * density.shape[1]
    smem = pl.BlockSpec(memory_space=pltpu.SMEM)
    vmem = pl.BlockSpec(memory_space=pltpu.VMEM)
    hbm = pl.BlockSpec(memory_space=pl.ANY)
    dma = pltpu.SemaphoreType.DMA
    steps, both, peers = dma((2, STEPS)), dma((2,)), dma((GROUPS,))
    finals, grad = pl.pallas_call(
        evolve_kernel,
        out_shape=(jax.ShapeDtypeStruct(fwd_fields.shape, f32), jax.ShapeDtypeStruct((rows, width_y), f32)),
        in_specs=[smem] * 5 + [vmem, hbm, hbm],
        out_specs=(hbm, vmem),
        scratch_shapes=[
            pltpu.VMEM((2, 6, depth, width_x + 2 * PAD, width_y), f32),
            pltpu.VMEM((depth, *layer), f32),
            pltpu.VMEM((depth, *layer), f32),
            pltpu.VMEM((2, STEPS, 3, width_x + PAD, width_y), f32),
            pltpu.VMEM((2, STEPS, 2, *layer), f32),
            pltpu.VMEM((2, 2, *layer), f32),
            pltpu.VMEM((2, 2, *layer), f32),
            pltpu.VMEM((2, STEPS, 3, *layer), f32),
            pltpu.VMEM((2, STEPS, 2, *layer), f32),
            pltpu.VMEM((STEPS, *layer), f32),
            pltpu.VMEM((2, STEPS, *layer), f32),
            pltpu.VMEM((2, *layer), f32),
            pltpu.VMEM((GROUPS * OWN, width_y), f32),
            pltpu.VMEM((GROUPS * OWN, width_y), f32),
            pltpu.VMEM((GROUPS * OWN, width_y), f32),
            pltpu.VMEM(layer, f32),
            pltpu.VMEM(layer, f32),
            pltpu.VMEM(layer, f32),
            both, dma(()),
            steps, steps, steps, steps, both, both, both, both, steps, steps, steps, steps,
            steps, steps, both, both, peers, peers, peers, peers, peers, peers,
        ],
        compiler_params=pltpu.CompilerParams(collective_id=0, has_side_effects=True, vmem_limit_bytes=48 << 20),
        name="evolve",
    )(source_pos, wave_idx, block_ids, material_idx, material_eps, density.reshape(rows, width_y), fwd_fields, adj_fields)
    return finals, grad.reshape(density.shape)


def solution(mesh):
    placed = (
        P("grp", None, "slab", None, None),
        P("grp", None, "slab", None, None),
        P("slab", "grp", None),
        P(),
        P(),
        P(),
        P("grp", None),
        P("grp"),
    )
    return jax.shard_map(
        per_device,
        mesh=mesh,
        in_specs=placed,
        out_specs=(P("grp", None, "slab", None, None), P("slab", "grp", None)),
        check_vma=False,
    )
```

```python
import math

import jax
import jax.numpy as jnp
from jax import lax
from jax.experimental import pallas as pl
from jax.experimental.pallas import tpu as pltpu
from jax.sharding import PartitionSpec as P

STEPS = 4
COURANT = 0.5
AMPLITUDE = 4.0
MESH = pl.DeviceIdType.MESH
ROWS = 32
PAD = 8
GROUPS = 32
OWN = 32
INNER = 24


def evolve_kernel(
    pos_hbm, wave_hbm, ids_hbm, mat_hbm, eps_hbm, dens_ref, fwd_ref, adj_ref, out_ref, grad_ref,
    st, coef_ref, tot_ref, pin, eu, pout, sdn, drv, gath, sendb, recvb, wmat, wtr, base,
    pos_ref, wave_ref, ids_ref, mat_ref, eps_ref,
    small_sem, load_sem, store_sem, u_s, u_r, d_s, d_r, ga_s, ga_r, ri_s, ri_r, rb_s, rb_r,
):
    depth, width_x, width_y = coef_ref.shape
    top = depth - 1
    grp, slab = lax.axis_index("grp"), lax.axis_index("slab")
    slabs = lax.axis_size("slab")
    has_up, has_dn = slab < slabs - 1, slab > 0
    inner = pl.ds(PAD, width_x)
    fields = (fwd_ref, adj_ref)

    def copy_to(src, dst, send, recv, to_slab):
        return pltpu.make_async_remote_copy(
            src_ref=src, dst_ref=dst, send_sem=send, recv_sem=recv, device_id=(grp, to_slab), device_id_type=MESH)

    def up_copy(ev, n):
        return copy_to(pout.at[ev, n], pin.at[ev, n], u_s.at[ev, n], u_r.at[ev, n], slab + 1)

    def dn_copy(ev, n, src):
        return copy_to(src, eu.at[ev, n], d_s.at[ev, n], d_r.at[ev, n], slab - 1)

    def peer_copy(src, dst, send, recv, peer):
        return pltpu.make_async_remote_copy(
            src_ref=src, dst_ref=dst, send_sem=send, recv_sem=recv, device_id=(peer, slab), device_id_type=MESH)

    def peer_of(d):
        return lax.rem(grp + d, GROUPS)

    def own_rows(k, first, count):
        return pl.ds(pl.multiple_of(k * OWN + first, 8), count)

    def gather_copy(d):
        return peer_copy(dens_ref, gath.at[own_rows(grp, 0, OWN), :], ga_s.at[d], ga_r.at[grp], peer_of(d))

    def sums_copy(d, first, count, send, recv):
        return peer_copy(sendb.at[own_rows(peer_of(d), first, count), :], recvb.at[own_rows(grp, first, count), :],
                         send.at[d], recv.at[grp], peer_of(d))

    barrier = pltpu.get_barrier_semaphore()

    @pl.loop(1, GROUPS)
    def _(d):
        pl.semaphore_signal(barrier, inc=1, device_id=(peer_of(d), slab), device_id_type=MESH)

    def greet(cond, to_slab):
        @pl.when(cond)
        def _():
            pl.semaphore_signal(barrier, inc=1, device_id=(grp, to_slab), device_id_type=MESH)

    greet(has_up, slab + 1)
    greet(has_dn, slab - 1)
    smalls = [
        pltpu.make_async_copy(src, dst, small_sem.at[i])
        for i, (src, dst) in enumerate(
            ((pos_hbm, pos_ref), (wave_hbm, wave_ref), (ids_hbm, ids_ref), (mat_hbm, mat_ref), (eps_hbm, eps_ref))
        )
    ]
    for copy in smalls:
        copy.start()
    for ev in range(2):
        pltpu.make_async_copy(fields[ev].at[0], st.at[ev, :, :, inner, :], load_sem.at[ev]).start()

    zeros = jnp.zeros((PAD, width_y), jnp.float32)

    @pl.loop(0, depth)
    def _(z):
        for ev in range(2):
            for c in (1, 2):
                st[ev, c, z, PAD + width_x :, :] = zeros
            for c in (4, 5):
                st[ev, c, z, :PAD, :] = zeros

    for copy in smalls:
        copy.wait()
    row = lax.broadcasted_iota(jnp.int32, (width_x, width_y), 0)
    col = lax.broadcasted_iota(jnp.int32, (width_x, width_y), 1)
    dx = (row - pos_ref[0, 1]).astype(jnp.float32) / (width_x / 4.0)
    dy = (col - pos_ref[0, 2]).astype(jnp.float32) / (width_y / 4.0)
    profile = jnp.exp(-0.5 * (dx * dx + dy * dy))
    wave = jnp.full((8, width_y), wave_ref[0], jnp.int32).astype(jnp.float32)
    omega = 2.0 * math.pi / (6.0 + 2.0 * wave)
    for n in range(STEPS):
        drv[n] = (AMPLITUDE * jnp.sin(omega * (n + 1.0)))[:1] * profile

    blocks = ids_ref.shape[0]
    block_rows = width_x // blocks
    slot = lax.rem(col, blocks)
    target = col // blocks
    for k in range(blocks):
        target = target + jnp.where(slot == k, ids_ref[k] * block_rows, 0)
    apart = jnp.abs(row - target)
    weights = jnp.where(apart == 0, 0.5, jnp.where(apart == 1, 0.25, 0.0))
    wmat[...] = jnp.concatenate([weights, weights], axis=1).astype(jnp.bfloat16)
    wtr[...] = jnp.concatenate([weights.T, weights.T], axis=1).astype(jnp.bfloat16)
    part = lax.broadcasted_iota(jnp.int32, (8, width_y), 0) // block_rows
    per_tile = 8 // block_rows
    for tile in range(width_x // 8):
        value = jnp.zeros((8, width_y), jnp.float32)
        for q in range(per_tile):
            value = jnp.where(part == q, eps_ref[mat_ref[tile * per_tile + q]], value)
        base[8 * tile : 8 * tile + 8, :] = value
    lane = lax.broadcasted_iota(jnp.int32, (ROWS, width_y), 1)
    is_first, is_last = lane == 0, lane == width_y - 1

    @pl.when(jnp.logical_not(has_up))
    def _():
        eu[...] = jnp.zeros_like(eu)

    @pl.when(jnp.logical_not(has_dn))
    def _():
        pin[...] = jnp.zeros_like(pin)

    own = pl.ds(pl.multiple_of(grp * OWN, 8), OWN)
    gath[own, :] = dens_ref[...]
    def next_y(v):
        return jnp.where(is_last, 0.0, pltpu.roll(v, width_y - 1, axis=1))

    def prev_y(v):
        return jnp.where(is_first, 0.0, pltpu.roll(v, 1, axis=1))

    def chunks():
        return [(r, pl.ds(PAD + r, ROWS)) for r in range(0, width_x, ROWS)]

    def h_layer(ev, z, above):
        for r, here in chunks():
            ahead = pl.ds(PAD + r + 1, ROWS)
            ex, ey, ez = (st[ev, c, z, here, :] for c in range(3))
            exu, eyu = above(r)
            dyz = next_y(ez) - ez
            dyx = next_y(ex) - ex
            st[ev, 3, z, here, :] += -COURANT * (dyz - (eyu - ey))
            st[ev, 4, z, here, :] += -COURANT * ((exu - ex) - (st[ev, 2, z, ahead, :] - ez))
            st[ev, 5, z, here, :] += -COURANT * ((st[ev, 1, z, ahead, :] - ey) - dyx)

    def top_part(ev, n):
        for r, here in chunks():
            ahead = pl.ds(PAD + r + 1, ROWS)
            ex, ey, ez = (st[ev, c, top, here, :] for c in range(3))
            out = pl.ds(r, ROWS)
            pout[ev, n, 0, out, :] = st[ev, 3, top, here, :] - COURANT * ((next_y(ez) - ez) + ey)
            pout[ev, n, 1, out, :] = st[ev, 4, top, here, :] + COURANT * ((st[ev, 2, top, ahead, :] - ez) + ex)

    def h_top(ev, n):
        for r, here in chunks():
            ahead = pl.ds(PAD + r + 1, ROWS)
            out = pl.ds(r, ROWS)
            ex, ey = (st[ev, c, top, here, :] for c in range(2))
            st[ev, 3, top, here, :] = pout[ev, n, 0, out, :] + COURANT * eu[ev, n, 1, out, :]
            st[ev, 4, top, here, :] = pout[ev, n, 1, out, :] - COURANT * eu[ev, n, 0, out, :]
            st[ev, 5, top, here, :] += -COURANT * ((st[ev, 1, top, ahead, :] - ey) - (next_y(ex) - ex))

    for ev in range(2):
        pltpu.make_async_copy(fields[ev].at[0], st.at[ev, :, :, inner, :], load_sem.at[ev]).wait()
        top_part(ev, 0)
    pl.semaphore_wait(barrier, GROUPS - 1 + has_up.astype(jnp.int32) + has_dn.astype(jnp.int32))

    def send_first(ev):
        @pl.when(has_dn)
        def _():
            dn_copy(ev, 0, fields[ev].at[0, 0:2, 0]).start()

        @pl.when(has_up)
        def _():
            up_copy(ev, 0).start()

    send_first(0)

    @pl.loop(1, GROUPS)
    def _(d):
        gather_copy(d).start()

    send_first(1)

    def e_layer(ev, n, z, below, send=None):
        plane = jnp.where((slab * depth + z == pos_ref[0, 0]) & (ev == 0), 1.0, 0.0)
        for r, here in chunks():
            back = pl.ds(PAD + r - 1, ROWS)
            out = pl.ds(r, ROWS)
            hx, hy, hz = (st[ev, c, z, here, :] for c in range(3, 6))
            hxd, hyd = below(r)
            coef = coef_ref[z, out, :]
            ex = st[ev, 0, z, here, :] + coef * ((hz - prev_y(hz)) - (hy - hyd))
            ey = st[ev, 1, z, here, :] + coef * ((hx - hxd) - (hz - st[ev, 5, z, back, :]))
            ez = st[ev, 2, z, here, :] + coef * ((hy - st[ev, 4, z, back, :]) - (hx - prev_y(hx)))
            ez = ez + plane * drv[n, out, :]
            for c, v in enumerate((ex, ey, ez)):
                st[ev, c, z, here, :] = v
            if send is not None:
                for c in range(send.shape[0]):
                    send[c, out, :] = (ex, ey, ez)[c]

    def filter_y(v):
        left = jnp.where(col == 0, 0.0, pltpu.roll(v, 1, axis=1))
        right = jnp.where(col == width_y - 1, 0.0, pltpu.roll(v, width_y - 1, axis=1))
        return (left + 2.0 * v + right) * 0.25

    def mixed(w, v):
        head = v.astype(jnp.bfloat16)
        rest = (v - head.astype(jnp.float32)).astype(jnp.bfloat16)
        return jnp.dot(w[...], jnp.concatenate([head, rest], axis=0), preferred_element_type=jnp.float32)

    def h_inside(ev, z):
        h_layer(ev, z, lambda r: (st[ev, 0, z + 1, pl.ds(PAD + r, ROWS), :], st[ev, 1, z + 1, pl.ds(PAD + r, ROWS), :]))

    def below(ev, z):
        return lambda r: (st[ev, 3, z - 1, pl.ds(PAD + r, ROWS), :], st[ev, 4, z - 1, pl.ds(PAD + r, ROWS), :])

    def add_total(n, z):
        for r, here in chunks():
            out = pl.ds(r, ROWS)
            new = sum(st[0, c, z, here, :] * st[1, c, z, here, :] for c in range(3))
            tot_ref[z, out, :] = jnp.where(n == 0, 0.0, tot_ref[z, out, :]) + new

    def make_coef():
        @pl.loop(1, GROUPS)
        def _(d):
            src = peer_of(d)
            peer_copy(dens_ref, gath.at[own_rows(src, 0, OWN), :], ga_s.at[d], ga_r.at[src], src).wait_recv()

        @pl.loop(0, depth)
        def _(z):
            rows = jnp.concatenate(
                [gath[pl.ds(z * block_rows + j, blocks, stride=OWN), :] for j in range(block_rows)], axis=0
            )
            smooth = mixed(wmat, filter_y(rows))
            coef_ref[z] = 0.5 / (base[...] + 3.0 * smooth)

    scale = 3.0 / (STEPS * math.sqrt(GROUPS))

    def pack_sums(z, place):
        back = mixed(wtr, filter_y(tot_ref[z])) * scale
        for j in range(block_rows):
            sendb[pl.ds(place * block_rows + j, blocks, stride=OWN), :] = back[j * blocks : (j + 1) * blocks]

    half = jnp.where(has_dn, COURANT, 0.0)

    def below_first(ev, n):
        def values(r):
            out, here = pl.ds(r, ROWS), pl.ds(PAD + r, ROWS)
            return (pin[ev, n, 0, out, :] + half * st[ev, 1, 0, here, :], pin[ev, n, 1, out, :] - half * st[ev, 0, 0, here, :])

        return values

    def edges(ev, n, sending):
        @pl.when(has_up)
        def _():
            dn_copy(ev, n, sdn.at[ev, n]).wait_recv()

        h_top(ev, n)
        e_layer(ev, n, top, below(ev, top))
        if sending:
            top_part(ev, n + 1)

            @pl.when(has_up)
            def _():
                up_copy(ev, n + 1).start()

        @pl.when(has_dn)
        def _():
            up_copy(ev, n).wait_recv()

        e_layer(ev, n, 0, below_first(ev, n), sdn.at[ev, n])
        if sending:

            @pl.when(has_dn)
            def _():
                dn_copy(ev, n + 1, sdn.at[ev, n]).start()

    @pl.loop(0, 2 * STEPS)
    def _(i):
        n, ev = i // 2, lax.rem(i, 2)

        h_inside(ev, 0)
        h_inside(ev, top - 1)

        @pl.when(i == 0)
        def _():
            make_coef()

        @pl.when(n < STEPS - 1)
        def _():
            edges(ev, n, True)

        @pl.loop(1, top - 1)
        def _(z):
            h_inside(ev, z)

        @pl.loop(1, top)
        def _(z):
            e_layer(ev, n, z, below(ev, z))

        @pl.when(ev == 1)
        def _():
            @pl.loop(1, top)
            def _(z):
                add_total(n, z)

        @pl.when(i == 2 * STEPS - 1)
        def _():
            @pl.loop(1, top)
            def _(z):
                pack_sums(z, z - 1)

            @pl.loop(1, GROUPS)
            def _(d):
                sums_copy(d, 0, INNER, ri_s, ri_r).start()

        @pl.when(n == STEPS - 1)
        def _():
            edges(ev, n, False)

        @pl.when(ev == 1)
        def _():
            add_total(n, 0)
            add_total(n, top)

        @pl.when(i == 2 * STEPS - 2)
        def _():
            pltpu.make_async_copy(st.at[0, :, :, inner, :], out_ref.at[0], store_sem).start()

    pack_sums(0, top - 1)
    pack_sums(top, top)

    @pl.loop(1, GROUPS)
    def _(d):
        sums_copy(d, INNER, OWN - INNER, rb_s, rb_r).start()

    def arrived(first, count, send, recv):
        def add(d, acc):
            src = peer_of(d)
            rows = own_rows(src, first, count)
            peer_copy(sendb.at[rows, :], recvb.at[rows, :], send.at[d], recv.at[src], src).wait_recv()
            return acc + recvb[rows, :]

        return lax.fori_loop(1, GROUPS, add, sendb[own_rows(grp, first, count), :])

    middle = arrived(0, INNER, ri_s, ri_r)
    for z in range(1, top):
        grad_ref[z * block_rows : (z + 1) * block_rows, :] = middle[(z - 1) * block_rows : z * block_rows]
    ends = arrived(INNER, OWN - INNER, rb_s, rb_r)
    grad_ref[0:block_rows, :] = ends[:block_rows]
    grad_ref[top * block_rows : depth * block_rows, :] = ends[block_rows:]

    pltpu.make_async_copy(st.at[0, :, :, inner, :], out_ref.at[0], store_sem).wait()

    @pl.loop(1, GROUPS)
    def _(d):
        gather_copy(d).wait_send()
        sums_copy(d, 0, INNER, ri_s, ri_r).wait_send()
        sums_copy(d, INNER, OWN - INNER, rb_s, rb_r).wait_send()

    @pl.loop(0, 2)
    def _(ev):
        @pl.loop(0, STEPS)
        def _(n):
            @pl.when(has_up)
            def _():
                up_copy(ev, n).wait_send()

            @pl.when(has_dn)
            def _():
                dn_copy(ev, n, sdn.at[ev, n]).wait_send()


def per_device(
    fwd_fields, adj_fields, density, block_ids, material_idx, material_eps, source_pos, wave_idx
):
    depth, width_x, width_y = fwd_fields.shape[2:]
    f32 = jnp.float32
    layer = (width_x, width_y)
    rows = density.shape[0] * density.shape[1]
    vmem = pl.BlockSpec(memory_space=pltpu.VMEM)
    hbm = pl.BlockSpec(memory_space=pl.ANY)
    dma = pltpu.SemaphoreType.DMA
    steps, peers = dma((2, STEPS)), dma((GROUPS,))
    finals, grad = pl.pallas_call(
        evolve_kernel,
        out_shape=(jax.ShapeDtypeStruct(fwd_fields.shape, f32), jax.ShapeDtypeStruct((rows, width_y), f32)),
        in_specs=[hbm] * 5 + [vmem, hbm, hbm],
        out_specs=(hbm, vmem),
        scratch_shapes=[
            pltpu.VMEM((2, 6, depth, width_x + 2 * PAD, width_y), f32),
            pltpu.VMEM((depth, *layer), f32),
            pltpu.VMEM((depth, *layer), f32),
            pltpu.VMEM((2, STEPS, 2, *layer), f32),
            pltpu.VMEM((2, STEPS, 2, *layer), f32),
            pltpu.VMEM((2, STEPS, 2, *layer), f32),
            pltpu.VMEM((2, STEPS, 2, *layer), f32),
            pltpu.VMEM((STEPS, *layer), f32),
            pltpu.VMEM((GROUPS * OWN, width_y), f32),
            pltpu.VMEM((GROUPS * OWN, width_y), f32),
            pltpu.VMEM((GROUPS * OWN, width_y), f32),
            pltpu.VMEM((width_x, 2 * width_x), jnp.bfloat16),
            pltpu.VMEM((width_x, 2 * width_x), jnp.bfloat16),
            pltpu.VMEM(layer, f32),
            *(pltpu.SMEM(a.shape, a.dtype) for a in (source_pos, wave_idx, block_ids, material_idx, material_eps)),
            dma((5,)), dma((2,)), dma(()), steps, steps, steps, steps, *[peers] * 6,
        ],
        compiler_params=pltpu.CompilerParams(collective_id=0, has_side_effects=True, vmem_limit_bytes=48 << 20),
        name="evolve",
    )(source_pos, wave_idx, block_ids, material_idx, material_eps, density.reshape(rows, width_y), fwd_fields, adj_fields)
    return finals, grad.reshape(density.shape)


def solution(mesh):
    placed = (
        P("grp", None, "slab", None, None),
        P("grp", None, "slab", None, None),
        P("slab", "grp", None),
        P(),
        P(),
        P(),
        P("grp", None),
        P("grp"),
    )
    return jax.shard_map(
        per_device,
        mesh=mesh,
        in_specs=placed,
        out_specs=(P("grp", None, "slab", None, None), P("slab", "grp", None)),
        check_vma=False,
    )
```

```python
import math

import jax
import jax.numpy as jnp
from jax import lax
from jax.experimental import pallas as pl
from jax.experimental.pallas import tpu as pltpu
from jax.sharding import PartitionSpec as P

STEPS = 4
COURANT = 0.5
AMPLITUDE = 4.0
MESH = pl.DeviceIdType.MESH
ROWS = 32
PAD = 8
GROUPS = 32
OWN = 32
INNER = 24
EDGE = 8
LINE = 8
COLUMNS = 4


def evolve_kernel(
    pos_hbm, wave_hbm, ids_hbm, mat_hbm, eps_hbm, dens_ref, fwd_ref, adj_ref, out_ref, grad_ref,
    st, coef_ref, tot_ref, pin, eu, pout, sdn, rel, drv, gath, mine, column, line, edge, edge_in, wmat, wtr, base,
    pos_ref, wave_ref, ids_ref, mat_ref, eps_ref,
    small_sem, load_sem, store_sem, own_sem, u1_s, u1_r, u2_s, u2_r, d1_s, d1_r, d2_s, d2_r, rl_s, rl_r,
    gl_s, gl_r, gc_s, gc_r, sc_s, sc_r, sl_s, sl_r, se_s, se_r,
):
    depth, width_x, width_y = coef_ref.shape
    top = depth - 1
    grp, slab = lax.axis_index("grp"), lax.axis_index("slab")
    slabs = lax.axis_size("slab")
    last = slabs - 1
    low, high = slabs // 2 - 1, slabs // 2
    has_up, has_dn = slab < last, slab > 0
    run, col_x, core = grp // LINE, lax.rem(grp // 2, COLUMNS), lax.rem(grp, 2)
    place = run * 2 + core
    far_low, far_high = slab == low, slab == high
    relay_up, relay_dn = slab == 0, slab == last
    inner = pl.ds(PAD, width_x)
    fields = (fwd_ref, adj_ref)

    def copy_to(src, dst, send, recv, to_slab):
        return pltpu.make_async_remote_copy(
            src_ref=src, dst_ref=dst, send_sem=send, recv_sem=recv, device_id=(grp, to_slab), device_id_type=MESH)

    def u1(ev, n):
        return copy_to(pout.at[ev, n, 0], pin.at[ev, n, 0], u1_s.at[ev, n], u1_r.at[ev, n], slab + 1)

    def u2(ev, n):
        return copy_to(pout.at[ev, n, 1], pin.at[ev, n, 1], u2_s.at[ev, n], u2_r.at[ev, n], slab + 1)

    def u2_via(ev, n):
        return copy_to(pout.at[ev, n, 1], rel.at[ev, n], u2_s.at[ev, n], rl_r.at[ev, n], 0)

    def relay_u2(ev, n):
        return copy_to(rel.at[ev, n], pin.at[ev, n, 1], rl_s.at[ev, n], u2_r.at[ev, n], high)

    def d1(ev, n, src):
        return copy_to(src, eu.at[ev, n, 0], d1_s.at[ev, n], d1_r.at[ev, n], slab - 1)

    def d2(ev, n, src):
        return copy_to(src, eu.at[ev, n, 1], d2_s.at[ev, n], d2_r.at[ev, n], slab - 1)

    def d2_via(ev, n, src):
        return copy_to(src, rel.at[ev, n], d2_s.at[ev, n], rl_r.at[ev, n], last)

    def relay_d2(ev, n):
        return copy_to(rel.at[ev, n], eu.at[ev, n, 1], rl_s.at[ev, n], d2_r.at[ev, n], low)

    def send_up(ev, n):
        @pl.when(has_up)
        def _():
            @pl.when(far_low)
            def _():
                u2_via(ev, n).start()

            @pl.when(jnp.logical_not(far_low))
            def _():
                u2(ev, n).start()

            u1(ev, n).start()

    def send_dn(ev, n, first, second):
        @pl.when(has_dn)
        def _():
            @pl.when(far_high)
            def _():
                d2_via(ev, n, second).start()

            @pl.when(jnp.logical_not(far_high))
            def _():
                d2(ev, n, second).start()

            d1(ev, n, first).start()

    def forward(ev, n):
        @pl.when(relay_up)
        def _():
            u2_via(ev, n).wait_recv()
            relay_u2(ev, n).start()

        @pl.when(relay_dn)
        def _():
            d2_via(ev, n, rel.at[ev, n]).wait_recv()
            relay_d2(ev, n).start()

    def peer_copy(src, dst, send, recv, peer):
        return pltpu.make_async_remote_copy(
            src_ref=src, dst_ref=dst, send_sem=send, recv_sem=recv, device_id=(peer, slab), device_id_type=MESH)

    def peer_of(d):
        return lax.rem(grp + d, GROUPS)

    def rows_of(k, count):
        return pl.ds(pl.multiple_of(k * count, 8), count)

    def slot_of(g):
        return lax.rem(g // 2, COLUMNS) * LINE + (g // LINE) * 2 + lax.rem(g, 2)

    def line_peer(q):
        other = lax.rem(place + q, LINE)
        return other, (other // 2) * LINE + col_x * 2 + lax.rem(other, 2)

    def column_peer(p):
        other = lax.rem(col_x + p, COLUMNS)
        return other, run * LINE + other * 2 + core

    def gather_line(q, sender):
        rows = gath.at[rows_of(col_x * LINE + sender, OWN), :]
        return peer_copy(dens_ref, rows, gl_s.at[q], gl_r.at[sender], line_peer(q)[1])

    def gather_column(p, sender):
        rows = gath.at[rows_of(sender, LINE * OWN), :]
        return peer_copy(rows, rows, gc_s.at[p], gc_r.at[sender], column_peer(p)[1])

    def sums_column(p, sender):
        other, peer = column_peer(p)
        return peer_copy(mine.at[rows_of(other, LINE * INNER), :], column.at[rows_of(sender, LINE * INNER), :],
                         sc_s.at[p], sc_r.at[sender], peer)

    def sums_line(q, sender):
        other, peer = line_peer(q)
        kept = rows_of(col_x * LINE + other, INNER)
        return peer_copy(mine.at[kept, :], line.at[rows_of(sender, INNER), :], sl_s.at[q], sl_r.at[sender], peer)

    def sums_edge(d, sender):
        peer = peer_of(d)
        return peer_copy(edge.at[rows_of(slot_of(peer), EDGE), :], edge_in.at[rows_of(slot_of(sender), EDGE), :],
                         se_s.at[d], se_r.at[sender], peer)

    barrier = pltpu.get_barrier_semaphore()

    @pl.loop(1, GROUPS)
    def _(d):
        pl.semaphore_signal(barrier, inc=1, device_id=(peer_of(d), slab), device_id_type=MESH)

    def greet(cond, to_slab):
        @pl.when(cond)
        def _():
            pl.semaphore_signal(barrier, inc=1, device_id=(grp, to_slab), device_id_type=MESH)

    greet(has_up, slab + 1)
    greet(has_dn, slab - 1)
    greet(far_low | far_high, 0)
    greet(far_low | far_high, last)
    greet(relay_up | relay_dn, low)
    greet(relay_up | relay_dn, high)
    smalls = [
        pltpu.make_async_copy(src, dst, small_sem.at[i])
        for i, (src, dst) in enumerate(
            ((pos_hbm, pos_ref), (wave_hbm, wave_ref), (ids_hbm, ids_ref), (mat_hbm, mat_ref), (eps_hbm, eps_ref))
        )
    ]
    for copy in smalls:
        copy.start()
    own_copy = pltpu.make_async_copy(dens_ref, gath.at[rows_of(slot_of(grp), OWN), :], own_sem)
    own_copy.start()
    for ev in range(2):
        pltpu.make_async_copy(fields[ev].at[0], st.at[ev, :, :, inner, :], load_sem.at[ev]).start()

    zeros = jnp.zeros((PAD, width_y), jnp.float32)

    @pl.loop(0, depth)
    def _(z):
        for ev in range(2):
            for c in (1, 2):
                st[ev, c, z, PAD + width_x :, :] = zeros
            for c in (4, 5):
                st[ev, c, z, :PAD, :] = zeros

    for copy in smalls:
        copy.wait()
    row = lax.broadcasted_iota(jnp.int32, (width_x, width_y), 0)
    col = lax.broadcasted_iota(jnp.int32, (width_x, width_y), 1)
    dx = (row - pos_ref[0, 1]).astype(jnp.float32) / (width_x / 4.0)
    dy = (col - pos_ref[0, 2]).astype(jnp.float32) / (width_y / 4.0)
    profile = jnp.exp(-0.5 * (dx * dx + dy * dy))
    wave = jnp.full((8, width_y), wave_ref[0], jnp.int32).astype(jnp.float32)
    omega = 2.0 * math.pi / (6.0 + 2.0 * wave)
    for n in range(STEPS):
        drv[n] = (AMPLITUDE * jnp.sin(omega * (n + 1.0)))[:1] * profile

    blocks = ids_ref.shape[0]
    block_rows = width_x // blocks
    slot = lax.rem(col, blocks)
    target = col // blocks
    for k in range(blocks):
        here = (k // 2 % COLUMNS) * LINE + (k // LINE) * 2 + k % 2
        target = target + jnp.where(slot == here, ids_ref[k] * block_rows, 0)
    apart = jnp.abs(row - target)
    weights = jnp.where(apart == 0, 0.5, jnp.where(apart == 1, 0.25, 0.0))
    wmat[...] = jnp.concatenate([weights, weights], axis=1).astype(jnp.bfloat16)
    wtr[...] = jnp.concatenate([weights.T, weights.T], axis=1).astype(jnp.bfloat16)
    part = lax.broadcasted_iota(jnp.int32, (8, width_y), 0) // block_rows
    per_tile = 8 // block_rows
    for tile in range(width_x // 8):
        value = jnp.zeros((8, width_y), jnp.float32)
        for q in range(per_tile):
            value = jnp.where(part == q, eps_ref[mat_ref[tile * per_tile + q]], value)
        base[8 * tile : 8 * tile + 8, :] = value
    lane = lax.broadcasted_iota(jnp.int32, (ROWS, width_y), 1)
    is_first, is_last = lane == 0, lane == width_y - 1

    @pl.when(jnp.logical_not(has_up))
    def _():
        eu[...] = jnp.zeros_like(eu)

    @pl.when(jnp.logical_not(has_dn))
    def _():
        pin[...] = jnp.zeros_like(pin)

    def next_y(v):
        return jnp.where(is_last, 0.0, pltpu.roll(v, width_y - 1, axis=1))

    def prev_y(v):
        return jnp.where(is_first, 0.0, pltpu.roll(v, 1, axis=1))

    def chunks():
        return [(r, pl.ds(PAD + r, ROWS)) for r in range(0, width_x, ROWS)]

    def h_layer(ev, z, above):
        for r, here in chunks():
            ahead = pl.ds(PAD + r + 1, ROWS)
            ex, ey, ez = (st[ev, c, z, here, :] for c in range(3))
            exu, eyu = above(r)
            dyz = next_y(ez) - ez
            dyx = next_y(ex) - ex
            st[ev, 3, z, here, :] += -COURANT * (dyz - (eyu - ey))
            st[ev, 4, z, here, :] += -COURANT * ((exu - ex) - (st[ev, 2, z, ahead, :] - ez))
            st[ev, 5, z, here, :] += -COURANT * ((st[ev, 1, z, ahead, :] - ey) - dyx)

    def top_part(ev, n):
        for r, here in chunks():
            ahead = pl.ds(PAD + r + 1, ROWS)
            ex, ey, ez = (st[ev, c, top, here, :] for c in range(3))
            out = pl.ds(r, ROWS)
            pout[ev, n, 0, out, :] = st[ev, 3, top, here, :] - COURANT * ((next_y(ez) - ez) + ey)
            pout[ev, n, 1, out, :] = st[ev, 4, top, here, :] + COURANT * ((st[ev, 2, top, ahead, :] - ez) + ex)

    def h_top(ev, n):
        for r, here in chunks():
            ahead = pl.ds(PAD + r + 1, ROWS)
            out = pl.ds(r, ROWS)
            ex, ey = (st[ev, c, top, here, :] for c in range(2))
            st[ev, 3, top, here, :] = pout[ev, n, 0, out, :] + COURANT * eu[ev, n, 1, out, :]
            st[ev, 4, top, here, :] = pout[ev, n, 1, out, :] - COURANT * eu[ev, n, 0, out, :]
            st[ev, 5, top, here, :] += -COURANT * ((st[ev, 1, top, ahead, :] - ey) - (next_y(ex) - ex))

    for ev in range(2):
        pltpu.make_async_copy(fields[ev].at[0], st.at[ev, :, :, inner, :], load_sem.at[ev]).wait()
        top_part(ev, 0)
    extra = jnp.where(far_low | far_high | relay_up | relay_dn, 2, 0)
    pl.semaphore_wait(barrier, GROUPS - 1 + has_up.astype(jnp.int32) + has_dn.astype(jnp.int32) + extra)

    @pl.loop(1, LINE)
    def _(q):
        gather_line(q, place).start()

    send_dn(0, 0, fwd_ref.at[0, 0, 0], fwd_ref.at[0, 1, 0])
    send_up(0, 0)

    def e_layer(ev, n, z, below, send=None):
        plane = jnp.where((slab * depth + z == pos_ref[0, 0]) & (ev == 0), 1.0, 0.0)
        for r, here in chunks():
            back = pl.ds(PAD + r - 1, ROWS)
            out = pl.ds(r, ROWS)
            hx, hy, hz = (st[ev, c, z, here, :] for c in range(3, 6))
            hxd, hyd = below(r)
            coef = coef_ref[z, out, :]
            ex = st[ev, 0, z, here, :] + coef * ((hz - prev_y(hz)) - (hy - hyd))
            ey = st[ev, 1, z, here, :] + coef * ((hx - hxd) - (hz - st[ev, 5, z, back, :]))
            ez = st[ev, 2, z, here, :] + coef * ((hy - st[ev, 4, z, back, :]) - (hx - prev_y(hx)))
            ez = ez + plane * drv[n, out, :]
            for c, v in enumerate((ex, ey, ez)):
                st[ev, c, z, here, :] = v
            if send is not None:
                for c in range(send.shape[0]):
                    send[c, out, :] = (ex, ey, ez)[c]

    def filter_y(v):
        left = jnp.where(col == 0, 0.0, pltpu.roll(v, 1, axis=1))
        right = jnp.where(col == width_y - 1, 0.0, pltpu.roll(v, width_y - 1, axis=1))
        return (left + 2.0 * v + right) * 0.25

    def mixed(w, v):
        head = v.astype(jnp.bfloat16)
        rest = (v - head.astype(jnp.float32)).astype(jnp.bfloat16)
        return jnp.dot(w[...], jnp.concatenate([head, rest], axis=0), preferred_element_type=jnp.float32)

    def h_inside(ev, z):
        h_layer(ev, z, lambda r: (st[ev, 0, z + 1, pl.ds(PAD + r, ROWS), :], st[ev, 1, z + 1, pl.ds(PAD + r, ROWS), :]))

    def below(ev, z):
        return lambda r: (st[ev, 3, z - 1, pl.ds(PAD + r, ROWS), :], st[ev, 4, z - 1, pl.ds(PAD + r, ROWS), :])

    def add_total(n, z):
        for r, here in chunks():
            out = pl.ds(r, ROWS)
            new = sum(st[0, c, z, here, :] * st[1, c, z, here, :] for c in range(3))
            tot_ref[z, out, :] = jnp.where(n == 0, 0.0, tot_ref[z, out, :]) + new

    def gather():
        own_copy.wait()

        @pl.loop(1, LINE)
        def _(q):
            gather_line(q, line_peer(q)[0]).wait_recv()

        @pl.loop(1, COLUMNS)
        def _(p):
            gather_column(p, col_x).start()

        send_dn(1, 0, adj_ref.at[0, 0, 0], adj_ref.at[0, 1, 0])
        send_up(1, 0)
        forward(0, 0)
        forward(1, 0)

        @pl.loop(1, COLUMNS)
        def _(p):
            gather_column(p, column_peer(p)[0]).wait_recv()

    def make_coef(z):
        rows = jnp.concatenate(
            [gath[pl.ds(z * block_rows + j, blocks, stride=OWN), :] for j in range(block_rows)], axis=0
        )
        coef_ref[z] = 0.5 / (base[...] + 3.0 * mixed(wmat, filter_y(rows)))

    scale = 3.0 / (STEPS * math.sqrt(GROUPS))

    def pack_sums(z, packed, first, count):
        back = mixed(wtr, filter_y(tot_ref[z])) * scale
        for j in range(block_rows):
            packed[pl.ds(first + j, blocks, stride=count), :] = back[j * blocks : (j + 1) * blocks]

    half = jnp.where(has_dn, COURANT, 0.0)

    def below_first(ev, n):
        def values(r):
            out, here = pl.ds(r, ROWS), pl.ds(PAD + r, ROWS)
            return (pin[ev, n, 0, out, :] + half * st[ev, 1, 0, here, :], pin[ev, n, 1, out, :] - half * st[ev, 0, 0, here, :])

        return values

    def edges(ev, n, sending):
        @pl.when(has_up)
        def _():
            d1(ev, n, sdn.at[ev, n, 0]).wait_recv()
            d2(ev, n, sdn.at[ev, n, 1]).wait_recv()

        h_top(ev, n)
        e_layer(ev, n, top, below(ev, top))
        if sending:
            top_part(ev, n + 1)
            send_up(ev, n + 1)

        @pl.when(has_dn)
        def _():
            u1(ev, n).wait_recv()
            u2(ev, n).wait_recv()

        e_layer(ev, n, 0, below_first(ev, n), sdn.at[ev, n])
        if sending:
            send_dn(ev, n + 1, sdn.at[ev, n, 0], sdn.at[ev, n, 1])

            @pl.when(n > 0)
            def _():
                forward(ev, n)

    def h_rest(ev):
        @pl.loop(0, top)
        def _(z):
            h_inside(ev, z)

    def e_rest(ev, n):
        @pl.loop(1, top)
        def _(z):
            e_layer(ev, n, z, below(ev, z))

    @pl.loop(0, 2 * STEPS - 2)
    def _(i):
        n, ev = i // 2, lax.rem(i, 2)
        h_rest(ev)

        @pl.when(i == 0)
        def _():
            gather()
            make_coef(0)
            make_coef(top)

        edges(ev, n, True)

        @pl.when(i == 0)
        def _():
            @pl.loop(1, top)
            def _(z):
                make_coef(z)

        e_rest(ev, n)

        @pl.when(ev == 1)
        def _():
            @pl.loop(0, depth)
            def _(z):
                add_total(n, z)

    n = STEPS - 1

    @pl.loop(0, 2)
    def _(ev):
        h_rest(ev)
        e_rest(ev, n)

    @pl.loop(1, top)
    def _(z):
        add_total(n, z)
        pack_sums(z, mine, (z - 1) * block_rows, INNER)

    @pl.loop(1, COLUMNS)
    def _(p):
        sums_column(p, col_x).start()

    @pl.loop(0, 2)
    def _(ev):
        forward(ev, n)
        edges(ev, n, False)

        @pl.when(ev == 0)
        def _():
            pltpu.make_async_copy(st.at[0, :, :, inner, :], out_ref.at[0], store_sem).start()

            @pl.loop(1, COLUMNS)
            def _(p):
                sender = column_peer(p)[0]
                sums_column(p, sender).wait_recv()
                kept = rows_of(col_x, LINE * INNER)
                mine[kept, :] += column[rows_of(sender, LINE * INNER), :]

            @pl.loop(1, LINE)
            def _(q):
                sums_line(q, place).start()

    add_total(n, 0)
    add_total(n, top)
    pack_sums(0, edge, 0, EDGE)
    pack_sums(top, edge, block_rows, EDGE)

    @pl.loop(1, GROUPS)
    def _(d):
        sums_edge(d, grp).start()

    def add_line(q, acc):
        sender = line_peer(q)[0]
        sums_line(q, sender).wait_recv()
        return acc + line[rows_of(sender, INNER), :]

    middle = lax.fori_loop(1, LINE, add_line, mine[rows_of(slot_of(grp), INNER), :])
    for z in range(1, top):
        grad_ref[z * block_rows : (z + 1) * block_rows, :] = middle[(z - 1) * block_rows : z * block_rows]

    def add_edge(d, acc):
        sender = peer_of(d)
        sums_edge(d, sender).wait_recv()
        return acc + edge_in[rows_of(slot_of(sender), EDGE), :]

    ends = lax.fori_loop(1, GROUPS, add_edge, edge[rows_of(slot_of(grp), EDGE), :])
    grad_ref[0:block_rows, :] = ends[:block_rows]
    grad_ref[top * block_rows : depth * block_rows, :] = ends[block_rows:]

    pltpu.make_async_copy(st.at[0, :, :, inner, :], out_ref.at[0], store_sem).wait()

    @pl.loop(1, LINE)
    def _(q):
        gather_line(q, place).wait_send()
        sums_line(q, place).wait_send()

    @pl.loop(1, COLUMNS)
    def _(p):
        gather_column(p, col_x).wait_send()
        sums_column(p, col_x).wait_send()

    @pl.loop(1, GROUPS)
    def _(d):
        sums_edge(d, grp).wait_send()

    @pl.loop(0, 2)
    def _(ev):
        @pl.loop(0, STEPS)
        def _(n):
            @pl.when(has_up)
            def _():
                u1(ev, n).wait_send()
                u2(ev, n).wait_send()

            @pl.when(has_dn)
            def _():
                d1(ev, n, sdn.at[ev, n, 0]).wait_send()
                d2(ev, n, sdn.at[ev, n, 1]).wait_send()

            @pl.when(relay_up)
            def _():
                relay_u2(ev, n).wait_send()

            @pl.when(relay_dn)
            def _():
                relay_d2(ev, n).wait_send()


def per_device(
    fwd_fields, adj_fields, density, block_ids, material_idx, material_eps, source_pos, wave_idx
):
    depth, width_x, width_y = fwd_fields.shape[2:]
    f32 = jnp.float32
    layer = (width_x, width_y)
    rows = density.shape[0] * density.shape[1]
    vmem = pl.BlockSpec(memory_space=pltpu.VMEM)
    anywhere = pl.BlockSpec(memory_space=pl.ANY)
    hbm = pl.BlockSpec(memory_space=pltpu.HBM)
    dma = pltpu.SemaphoreType.DMA
    steps = dma((2, STEPS))
    finals, grad = pl.pallas_call(
        evolve_kernel,
        out_shape=(jax.ShapeDtypeStruct(fwd_fields.shape, f32), jax.ShapeDtypeStruct((rows, width_y), f32)),
        in_specs=[hbm] * 8,
        out_specs=(anywhere, vmem),
        scratch_shapes=[
            pltpu.VMEM((2, 6, depth, width_x + 2 * PAD, width_y), f32),
            pltpu.VMEM((depth, *layer), f32),
            pltpu.VMEM((depth, *layer), f32),
            pltpu.VMEM((2, STEPS, 2, *layer), f32),
            pltpu.VMEM((2, STEPS, 2, *layer), f32),
            pltpu.VMEM((2, STEPS, 2, *layer), f32),
            pltpu.VMEM((2, STEPS, 2, *layer), f32),
            pltpu.VMEM((2, STEPS, *layer), f32),
            pltpu.VMEM((STEPS, *layer), f32),
            pltpu.VMEM((GROUPS * OWN, width_y), f32),
            pltpu.VMEM((GROUPS * INNER, width_y), f32),
            pltpu.VMEM((GROUPS * INNER, width_y), f32),
            pltpu.VMEM((LINE * INNER, width_y), f32),
            pltpu.VMEM((GROUPS * EDGE, width_y), f32),
            pltpu.VMEM((GROUPS * EDGE, width_y), f32),
            pltpu.VMEM((width_x, 2 * width_x), jnp.bfloat16),
            pltpu.VMEM((width_x, 2 * width_x), jnp.bfloat16),
            pltpu.VMEM(layer, f32),
            *(pltpu.SMEM(a.shape, a.dtype) for a in (source_pos, wave_idx, block_ids, material_idx, material_eps)),
            dma((5,)), dma((2,)), dma(()), dma(()), *[steps] * 10,
            *[dma((LINE,))] * 2, *[dma((COLUMNS,))] * 4, *[dma((LINE,))] * 2, *[dma((GROUPS,))] * 2,
        ],
        compiler_params=pltpu.CompilerParams(collective_id=0, has_side_effects=True, vmem_limit_bytes=48 << 20),
        name="evolve",
    )(source_pos, wave_idx, block_ids, material_idx, material_eps, density.reshape(rows, width_y), fwd_fields, adj_fields)
    return finals, grad.reshape(density.shape)


def solution(mesh):
    placed = (
        P("grp", None, "slab", None, None),
        P("grp", None, "slab", None, None),
        P("slab", "grp", None),
        P(),
        P(),
        P(),
        P("grp", None),
        P("grp"),
    )
    return jax.shard_map(
        per_device,
        mesh=mesh,
        in_specs=placed,
        out_specs=(P("grp", None, "slab", None, None), P("slab", "grp", None)),
        check_vma=False,
    )
```

```python
import math

import jax
import jax.numpy as jnp
from jax import lax
from jax.experimental import pallas as pl
from jax.experimental.pallas import tpu as pltpu
from jax.sharding import PartitionSpec as P

STEPS = 4
COURANT = 0.5
AMPLITUDE = 4.0
MESH = pl.DeviceIdType.MESH
ROWS = 32
PAD = 8
GROUPS = 32
OWN = 32
INNER = 24
EDGE = 8
LINE = 8
COLUMNS = 4


def evolve_kernel(
    pos_hbm, wave_hbm, ids_hbm, mat_hbm, eps_hbm, dens_ref, fwd_ref, adj_ref, out_ref, grad_ref,
    st, coef_ref, tot_ref, pin, eu, pout, sdn, rel, drv, gath, mine, column, line, edge, edge_in, wmat, wtr, base,
    pos_ref, wave_ref, ids_ref, mat_ref, eps_ref,
    small_sem, load_sem, store_sem, own_sem, u1_s, u1_r, u2_s, u2_r, d1_s, d1_r, d2_s, d2_r, rl_s, rl_r,
    gl_s, gl_r, gc_s, gc_r, sc_s, sc_r, sl_s, sl_r, se_s, se_r,
):
    depth, width_x, width_y = coef_ref.shape
    top = depth - 1
    grp, slab = lax.axis_index("grp"), lax.axis_index("slab")
    slabs = lax.axis_size("slab")
    last = slabs - 1
    low, high = slabs // 2 - 1, slabs // 2
    has_up, has_dn = slab < last, slab > 0
    run, col_x, core = grp // LINE, lax.rem(grp // 2, COLUMNS), lax.rem(grp, 2)
    place = run * 2 + core
    far_low, far_high = slab == low, slab == high
    relay_up, relay_dn = slab == 0, slab == last
    inner = pl.ds(PAD, width_x)
    fields = (fwd_ref, adj_ref)

    def copy_to(src, dst, send, recv, to_slab):
        return pltpu.make_async_remote_copy(
            src_ref=src, dst_ref=dst, send_sem=send, recv_sem=recv, device_id=(grp, to_slab), device_id_type=MESH)

    def u1(ev, n):
        return copy_to(pout.at[ev, n, 0], pin.at[ev, n, 0], u1_s.at[ev, n], u1_r.at[ev, n], slab + 1)

    def u2(ev, n):
        return copy_to(pout.at[ev, n, 1], pin.at[ev, n, 1], u2_s.at[ev, n], u2_r.at[ev, n], slab + 1)

    def u2_via(ev, n):
        return copy_to(pout.at[ev, n, 1], rel.at[ev, n], u2_s.at[ev, n], rl_r.at[ev, n], 0)

    def relay_u2(ev, n):
        return copy_to(rel.at[ev, n], pin.at[ev, n, 1], rl_s.at[ev, n], u2_r.at[ev, n], high)

    def d1(ev, n, src):
        return copy_to(src, eu.at[ev, n, 0], d1_s.at[ev, n], d1_r.at[ev, n], slab - 1)

    def d2(ev, n, src):
        return copy_to(src, eu.at[ev, n, 1], d2_s.at[ev, n], d2_r.at[ev, n], slab - 1)

    def d2_via(ev, n, src):
        return copy_to(src, rel.at[ev, n], d2_s.at[ev, n], rl_r.at[ev, n], last)

    def relay_d2(ev, n):
        return copy_to(rel.at[ev, n], eu.at[ev, n, 1], rl_s.at[ev, n], d2_r.at[ev, n], low)

    def send_up(ev, n):
        @pl.when(has_up)
        def _():
            @pl.when(far_low)
            def _():
                u2_via(ev, n).start()

            @pl.when(jnp.logical_not(far_low))
            def _():
                u2(ev, n).start()

            u1(ev, n).start()

    def send_dn(ev, n, first, second):
        @pl.when(has_dn)
        def _():
            @pl.when(far_high)
            def _():
                d2_via(ev, n, second).start()

            @pl.when(jnp.logical_not(far_high))
            def _():
                d2(ev, n, second).start()

            d1(ev, n, first).start()

    def forward(ev, n):
        @pl.when(relay_up)
        def _():
            u2_via(ev, n).wait_recv()
            relay_u2(ev, n).start()

        @pl.when(relay_dn)
        def _():
            d2_via(ev, n, rel.at[ev, n]).wait_recv()
            relay_d2(ev, n).start()

    def peer_copy(src, dst, send, recv, peer):
        return pltpu.make_async_remote_copy(
            src_ref=src, dst_ref=dst, send_sem=send, recv_sem=recv, device_id=(peer, slab), device_id_type=MESH)

    def peer_of(d):
        return lax.rem(grp + d, GROUPS)

    def rows_of(k, count):
        return pl.ds(pl.multiple_of(k * count, 8), count)

    def slot_of(g):
        return lax.rem(g // 2, COLUMNS) * LINE + (g // LINE) * 2 + lax.rem(g, 2)

    def line_peer(q):
        other = lax.rem(place + q, LINE)
        return other, (other // 2) * LINE + col_x * 2 + lax.rem(other, 2)

    def column_peer(p):
        other = lax.rem(col_x + p, COLUMNS)
        return other, run * LINE + other * 2 + core

    def gather_line(q, sender):
        rows = gath.at[rows_of(col_x * LINE + sender, OWN), :]
        return peer_copy(dens_ref, rows, gl_s.at[q], gl_r.at[sender], line_peer(q)[1])

    def gather_column(p, sender, which, src=None):
        rows = gath.at[rows_of(sender * LINE + which, OWN), :]
        return peer_copy(rows if src is None else src, rows, gc_s.at[p, which], gc_r.at[sender, which], column_peer(p)[1])

    def sums_column(p, sender):
        other, peer = column_peer(p)
        return peer_copy(mine.at[rows_of(other, LINE * INNER), :], column.at[rows_of(sender, LINE * INNER), :],
                         sc_s.at[p], sc_r.at[sender], peer)

    def sums_line(q, sender):
        other, peer = line_peer(q)
        kept = rows_of(col_x * LINE + other, INNER)
        return peer_copy(mine.at[kept, :], line.at[rows_of(sender, INNER), :], sl_s.at[q], sl_r.at[sender], peer)

    def sums_edge(d, sender):
        peer = peer_of(d)
        return peer_copy(edge.at[rows_of(slot_of(peer), EDGE), :], edge_in.at[rows_of(slot_of(sender), EDGE), :],
                         se_s, se_r, peer)

    barrier = pltpu.get_barrier_semaphore()

    @pl.loop(1, GROUPS)
    def _(d):
        pl.semaphore_signal(barrier, inc=1, device_id=(peer_of(d), slab), device_id_type=MESH)

    def greet(cond, to_slab):
        @pl.when(cond)
        def _():
            pl.semaphore_signal(barrier, inc=1, device_id=(grp, to_slab), device_id_type=MESH)

    greet(has_up, slab + 1)
    greet(has_dn, slab - 1)
    greet(far_low | far_high, 0)
    greet(far_low | far_high, last)
    greet(relay_up | relay_dn, low)
    greet(relay_up | relay_dn, high)
    smalls = [
        pltpu.make_async_copy(src, dst, small_sem.at[i])
        for i, (src, dst) in enumerate(
            ((pos_hbm, pos_ref), (wave_hbm, wave_ref), (ids_hbm, ids_ref), (mat_hbm, mat_ref), (eps_hbm, eps_ref))
        )
    ]
    for copy in smalls:
        copy.start()
    own_copy = pltpu.make_async_copy(dens_ref, gath.at[rows_of(slot_of(grp), OWN), :], own_sem)
    own_copy.start()
    for ev in range(2):
        pltpu.make_async_copy(fields[ev].at[0], st.at[ev, :, :, inner, :], load_sem.at[ev]).start()

    zeros = jnp.zeros((PAD, width_y), jnp.float32)

    @pl.loop(0, depth)
    def _(z):
        for ev in range(2):
            for c in (1, 2):
                st[ev, c, z, PAD + width_x :, :] = zeros
            for c in (4, 5):
                st[ev, c, z, :PAD, :] = zeros

    for copy in smalls:
        copy.wait()
    row = lax.broadcasted_iota(jnp.int32, (width_x, width_y), 0)
    col = lax.broadcasted_iota(jnp.int32, (width_x, width_y), 1)
    dx = (row - pos_ref[0, 1]).astype(jnp.float32) / (width_x / 4.0)
    dy = (col - pos_ref[0, 2]).astype(jnp.float32) / (width_y / 4.0)
    profile = jnp.exp(-0.5 * (dx * dx + dy * dy))
    wave = jnp.full((8, width_y), wave_ref[0], jnp.int32).astype(jnp.float32)
    omega = 2.0 * math.pi / (6.0 + 2.0 * wave)
    for n in range(STEPS):
        drv[n] = (AMPLITUDE * jnp.sin(omega * (n + 1.0)))[:1] * profile

    blocks = ids_ref.shape[0]
    block_rows = width_x // blocks
    slot = lax.rem(col, blocks)
    target = col // blocks
    for k in range(blocks):
        here = (k // 2 % COLUMNS) * LINE + (k // LINE) * 2 + k % 2
        target = target + jnp.where(slot == here, ids_ref[k] * block_rows, 0)
    apart = jnp.abs(row - target)
    weights = jnp.where(apart == 0, 0.5, jnp.where(apart == 1, 0.25, 0.0))
    wmat[...] = jnp.concatenate([weights, weights], axis=1).astype(jnp.bfloat16)
    wtr[...] = jnp.concatenate([weights.T, weights.T], axis=1).astype(jnp.bfloat16)
    part = lax.broadcasted_iota(jnp.int32, (8, width_y), 0) // block_rows
    per_tile = 8 // block_rows
    for tile in range(width_x // 8):
        value = jnp.zeros((8, width_y), jnp.float32)
        for q in range(per_tile):
            value = jnp.where(part == q, eps_ref[mat_ref[tile * per_tile + q]], value)
        base[8 * tile : 8 * tile + 8, :] = value
    lane = lax.broadcasted_iota(jnp.int32, (ROWS, width_y), 1)
    is_first, is_last = lane == 0, lane == width_y - 1

    @pl.when(jnp.logical_not(has_up))
    def _():
        eu[...] = jnp.zeros_like(eu)

    @pl.when(jnp.logical_not(has_dn))
    def _():
        pin[...] = jnp.zeros_like(pin)

    def next_y(v):
        return jnp.where(is_last, 0.0, pltpu.roll(v, width_y - 1, axis=1))

    def prev_y(v):
        return jnp.where(is_first, 0.0, pltpu.roll(v, 1, axis=1))

    def chunks():
        return [(r, pl.ds(PAD + r, ROWS)) for r in range(0, width_x, ROWS)]

    def h_layer(ev, z, above):
        for r, here in chunks():
            ahead = pl.ds(PAD + r + 1, ROWS)
            ex, ey, ez = (st[ev, c, z, here, :] for c in range(3))
            exu, eyu = above(r)
            dyz = next_y(ez) - ez
            dyx = next_y(ex) - ex
            st[ev, 3, z, here, :] += -COURANT * (dyz - (eyu - ey))
            st[ev, 4, z, here, :] += -COURANT * ((exu - ex) - (st[ev, 2, z, ahead, :] - ez))
            st[ev, 5, z, here, :] += -COURANT * ((st[ev, 1, z, ahead, :] - ey) - dyx)

    def top_part(ev, n):
        for r, here in chunks():
            ahead = pl.ds(PAD + r + 1, ROWS)
            ex, ey, ez = (st[ev, c, top, here, :] for c in range(3))
            out = pl.ds(r, ROWS)
            pout[ev, n, 0, out, :] = st[ev, 3, top, here, :] - COURANT * ((next_y(ez) - ez) + ey)
            pout[ev, n, 1, out, :] = st[ev, 4, top, here, :] + COURANT * ((st[ev, 2, top, ahead, :] - ez) + ex)

    def h_top(ev, n):
        for r, here in chunks():
            ahead = pl.ds(PAD + r + 1, ROWS)
            out = pl.ds(r, ROWS)
            ex, ey = (st[ev, c, top, here, :] for c in range(2))
            st[ev, 3, top, here, :] = pout[ev, n, 0, out, :] + COURANT * eu[ev, n, 1, out, :]
            st[ev, 4, top, here, :] = pout[ev, n, 1, out, :] - COURANT * eu[ev, n, 0, out, :]
            st[ev, 5, top, here, :] += -COURANT * ((st[ev, 1, top, ahead, :] - ey) - (next_y(ex) - ex))

    for ev in range(2):
        pltpu.make_async_copy(fields[ev].at[0], st.at[ev, :, :, inner, :], load_sem.at[ev]).wait()
        top_part(ev, 0)
    extra = jnp.where(far_low | far_high | relay_up | relay_dn, 2, 0)
    pl.semaphore_wait(barrier, GROUPS - 1 + has_up.astype(jnp.int32) + has_dn.astype(jnp.int32) + extra)

    @pl.loop(1, LINE)
    def _(q):
        gather_line(q, place).start()

    @pl.loop(1, COLUMNS)
    def _(p):
        gather_column(p, col_x, place, dens_ref).start()

    send_dn(0, 0, fwd_ref.at[0, 0, 0], fwd_ref.at[0, 1, 0])
    send_up(0, 0)

    def e_layer(ev, n, z, below, send=None):
        plane = jnp.where((slab * depth + z == pos_ref[0, 0]) & (ev == 0), 1.0, 0.0)
        for r, here in chunks():
            back = pl.ds(PAD + r - 1, ROWS)
            out = pl.ds(r, ROWS)
            hx, hy, hz = (st[ev, c, z, here, :] for c in range(3, 6))
            hxd, hyd = below(r)
            coef = coef_ref[z, out, :]
            ex = st[ev, 0, z, here, :] + coef * ((hz - prev_y(hz)) - (hy - hyd))
            ey = st[ev, 1, z, here, :] + coef * ((hx - hxd) - (hz - st[ev, 5, z, back, :]))
            ez = st[ev, 2, z, here, :] + coef * ((hy - st[ev, 4, z, back, :]) - (hx - prev_y(hx)))
            ez = ez + plane * drv[n, out, :]
            for c, v in enumerate((ex, ey, ez)):
                st[ev, c, z, here, :] = v
            if send is not None:
                for c in range(send.shape[0]):
                    send[c, out, :] = (ex, ey, ez)[c]

    def filter_y(v):
        left = jnp.where(col == 0, 0.0, pltpu.roll(v, 1, axis=1))
        right = jnp.where(col == width_y - 1, 0.0, pltpu.roll(v, width_y - 1, axis=1))
        return (left + 2.0 * v + right) * 0.25

    def mixed(w, v):
        head = v.astype(jnp.bfloat16)
        rest = (v - head.astype(jnp.float32)).astype(jnp.bfloat16)
        return jnp.dot(w[...], jnp.concatenate([head, rest], axis=0), preferred_element_type=jnp.float32)

    def h_inside(ev, z):
        h_layer(ev, z, lambda r: (st[ev, 0, z + 1, pl.ds(PAD + r, ROWS), :], st[ev, 1, z + 1, pl.ds(PAD + r, ROWS), :]))

    def below(ev, z):
        return lambda r: (st[ev, 3, z - 1, pl.ds(PAD + r, ROWS), :], st[ev, 4, z - 1, pl.ds(PAD + r, ROWS), :])

    def add_total(n, z):
        for r, here in chunks():
            out = pl.ds(r, ROWS)
            new = sum(st[0, c, z, here, :] * st[1, c, z, here, :] for c in range(3))
            tot_ref[z, out, :] = jnp.where(n == 0, 0.0, tot_ref[z, out, :]) + new

    def gather():
        own_copy.wait()

        @pl.loop(1, LINE)
        def _(q):
            which = line_peer(q)[0]
            gather_line(q, which).wait_recv()

            @pl.loop(1, COLUMNS)
            def _(p):
                gather_column(p, col_x, which).start()

        send_dn(1, 0, adj_ref.at[0, 0, 0], adj_ref.at[0, 1, 0])
        send_up(1, 0)
        forward(0, 0)
        forward(1, 0)

        @pl.loop(0, LINE)
        def _(which):
            @pl.loop(1, COLUMNS)
            def _(p):
                gather_column(p, column_peer(p)[0], which).wait_recv()

    def make_coef(z):
        rows = jnp.concatenate(
            [gath[pl.ds(z * block_rows + j, blocks, stride=OWN), :] for j in range(block_rows)], axis=0
        )
        coef_ref[z] = 0.5 / (base[...] + 3.0 * mixed(wmat, filter_y(rows)))

    scale = 3.0 / (STEPS * math.sqrt(GROUPS))

    def pack_sums(z, packed, first, count):
        back = mixed(wtr, filter_y(tot_ref[z])) * scale
        for j in range(block_rows):
            packed[pl.ds(first + j, blocks, stride=count), :] = back[j * blocks : (j + 1) * blocks]

    half = jnp.where(has_dn, COURANT, 0.0)

    def below_first(ev, n):
        def values(r):
            out, here = pl.ds(r, ROWS), pl.ds(PAD + r, ROWS)
            return (pin[ev, n, 0, out, :] + half * st[ev, 1, 0, here, :], pin[ev, n, 1, out, :] - half * st[ev, 0, 0, here, :])

        return values

    def edges(ev, n, sending):
        @pl.when(has_up)
        def _():
            d1(ev, n, sdn.at[ev, n, 0]).wait_recv()
            d2(ev, n, sdn.at[ev, n, 1]).wait_recv()

        h_top(ev, n)
        e_layer(ev, n, top, below(ev, top))
        if sending:
            top_part(ev, n + 1)
            send_up(ev, n + 1)

        @pl.when(has_dn)
        def _():
            u1(ev, n).wait_recv()
            u2(ev, n).wait_recv()

        e_layer(ev, n, 0, below_first(ev, n), sdn.at[ev, n])
        if sending:
            send_dn(ev, n + 1, sdn.at[ev, n, 0], sdn.at[ev, n, 1])

    def h_rest(ev):
        h_inside(ev, 0)

        @pl.loop(1, top, step=2)
        def _(z):
            h_inside(ev, z)
            h_inside(ev, z + 1)

    def e_rest(ev, n):
        @pl.loop(1, top, step=2)
        def _(z):
            e_layer(ev, n, z, below(ev, z))
            e_layer(ev, n, z + 1, below(ev, z + 1))

    @pl.loop(0, 2 * STEPS - 2)
    def _(i):
        n, ev = i // 2, lax.rem(i, 2)
        h_rest(ev)

        @pl.when(i == 0)
        def _():
            gather()
            make_coef(0)
            make_coef(top)

        edges(ev, n, True)

        @pl.when(i == 0)
        def _():
            @pl.loop(1, top)
            def _(z):
                make_coef(z)

        e_rest(ev, n)

        @pl.when((i > 0) & (i < 2 * STEPS - 3))
        def _():
            forward(1 - ev, (i + 1) // 2)

        @pl.when(ev == 1)
        def _():
            @pl.loop(0, depth)
            def _(z):
                add_total(n, z)

    def settle():
        @pl.loop(1, LINE)
        def _(q):
            gather_line(q, place).wait_send()

        @pl.loop(1, COLUMNS)
        def _(p):
            sums_column(p, col_x).wait_send()

            @pl.loop(0, LINE)
            def _(which):
                gather_column(p, col_x, which).wait_send()

        @pl.loop(0, 2 * STEPS)
        def _(i):
            n, ev = i // 2, lax.rem(i, 2)

            @pl.when(has_up)
            def _():
                u1(ev, n).wait_send()
                u2(ev, n).wait_send()

            @pl.when(has_dn)
            def _():
                d1(ev, n, sdn.at[ev, n, 0]).wait_send()
                d2(ev, n, sdn.at[ev, n, 1]).wait_send()

            @pl.when(relay_up)
            def _():
                relay_u2(ev, n).wait_send()

            @pl.when(relay_dn)
            def _():
                relay_d2(ev, n).wait_send()

    n = STEPS - 1

    @pl.loop(0, 2)
    def _(ev):
        h_rest(ev)
        e_rest(ev, n)

        @pl.when(ev == 0)
        def _():
            forward(0, n)

    @pl.loop(1, top)
    def _(z):
        add_total(n, z)
        pack_sums(z, mine, (z - 1) * block_rows, INNER)

    @pl.loop(1, COLUMNS)
    def _(p):
        sums_column(p, col_x).start()

    forward(1, n)

    @pl.loop(0, 2)
    def _(ev):
        edges(ev, n, False)

        @pl.when(ev == 0)
        def _():
            pltpu.make_async_copy(st.at[0, :, :, inner, :], out_ref.at[0], store_sem).start()

            @pl.loop(1, COLUMNS)
            def _(p):
                sender = column_peer(p)[0]
                sums_column(p, sender).wait_recv()
                kept = rows_of(col_x, LINE * INNER)
                mine[kept, :] += column[rows_of(sender, LINE * INNER), :]

            @pl.loop(1, LINE)
            def _(q):
                sums_line(q, place).start()

            settle()

    add_total(n, 0)
    add_total(n, top)
    pack_sums(0, edge, 0, EDGE)
    pack_sums(top, edge, block_rows, EDGE)

    @pl.loop(1, GROUPS)
    def _(d):
        sums_edge(d, grp).start()

    def add_line(q, acc):
        sender = line_peer(q)[0]
        sums_line(q, sender).wait_recv()
        return acc + line[rows_of(sender, INNER), :]

    middle = lax.fori_loop(1, LINE, add_line, mine[rows_of(slot_of(grp), INNER), :])
    for z in range(1, top):
        grad_ref[z * block_rows : (z + 1) * block_rows, :] = middle[(z - 1) * block_rows : z * block_rows]

    others = pl.ds(0, (GROUPS - 1) * EDGE)
    all_edges = peer_copy(edge.at[others, :], edge_in.at[others, :], se_s, se_r, peer_of(1))
    edge_in[rows_of(slot_of(grp), EDGE), :] = edge[rows_of(slot_of(grp), EDGE), :]
    all_edges.wait_recv()
    ends = edge_in[0:EDGE, :]
    for other in range(1, GROUPS):
        ends = ends + edge_in[other * EDGE : (other + 1) * EDGE, :]
    grad_ref[0:block_rows, :] = ends[:block_rows]
    grad_ref[top * block_rows : depth * block_rows, :] = ends[block_rows:]

    pltpu.make_async_copy(st.at[0, :, :, inner, :], out_ref.at[0], store_sem).wait()

    @pl.loop(1, LINE)
    def _(q):
        sums_line(q, place).wait_send()

    all_edges.wait_send()


def per_device(
    fwd_fields, adj_fields, density, block_ids, material_idx, material_eps, source_pos, wave_idx
):
    depth, width_x, width_y = fwd_fields.shape[2:]
    f32 = jnp.float32
    layer = (width_x, width_y)
    rows = density.shape[0] * density.shape[1]
    vmem = pl.BlockSpec(memory_space=pltpu.VMEM)
    anywhere = pl.BlockSpec(memory_space=pl.ANY)
    hbm = pl.BlockSpec(memory_space=pltpu.HBM)
    dma = pltpu.SemaphoreType.DMA
    steps = dma((2, STEPS))
    def in_hbm(a):
        return pltpu.with_memory_space_constraint(a, pltpu.HBM)

    finals, grad = pl.pallas_call(
        evolve_kernel,
        out_shape=(jax.ShapeDtypeStruct(fwd_fields.shape, f32), jax.ShapeDtypeStruct((rows, width_y), f32)),
        in_specs=[hbm] * 8,
        out_specs=(anywhere, vmem),
        scratch_shapes=[
            pltpu.VMEM((2, 6, depth, width_x + 2 * PAD, width_y), f32),
            pltpu.VMEM((depth, *layer), f32),
            pltpu.VMEM((depth, *layer), f32),
            pltpu.VMEM((2, STEPS, 2, *layer), f32),
            pltpu.VMEM((2, STEPS, 2, *layer), f32),
            pltpu.VMEM((2, STEPS, 2, *layer), f32),
            pltpu.VMEM((2, STEPS, 2, *layer), f32),
            pltpu.VMEM((2, STEPS, *layer), f32),
            pltpu.VMEM((STEPS, *layer), f32),
            pltpu.VMEM((GROUPS * OWN, width_y), f32),
            pltpu.VMEM((GROUPS * INNER, width_y), f32),
            pltpu.VMEM((GROUPS * INNER, width_y), f32),
            pltpu.VMEM((LINE * INNER, width_y), f32),
            pltpu.VMEM((GROUPS * EDGE, width_y), f32),
            pltpu.VMEM((GROUPS * EDGE, width_y), f32),
            pltpu.VMEM((width_x, 2 * width_x), jnp.bfloat16),
            pltpu.VMEM((width_x, 2 * width_x), jnp.bfloat16),
            pltpu.VMEM(layer, f32),
            *(pltpu.SMEM(a.shape, a.dtype) for a in (source_pos, wave_idx, block_ids, material_idx, material_eps)),
            dma((5,)), dma((2,)), dma(()), dma(()), *[steps] * 10,
            *[dma((LINE,))] * 2, *[dma((COLUMNS, LINE))] * 2, *[dma((COLUMNS,))] * 2, *[dma((LINE,))] * 2, dma(()), dma(()),
        ],
        compiler_params=pltpu.CompilerParams(collective_id=0, has_side_effects=True, vmem_limit_bytes=48 << 20),
        name="evolve",
    )(in_hbm(source_pos), wave_idx, in_hbm(block_ids), in_hbm(material_idx), in_hbm(material_eps), in_hbm(density.reshape(rows, width_y)), fwd_fields, adj_fields)
    return finals, grad.reshape(density.shape)


def solution(mesh):
    placed = (
        P("grp", None, "slab", None, None),
        P("grp", None, "slab", None, None),
        P("slab", "grp", None),
        P(),
        P(),
        P(),
        P("grp", None),
        P("grp"),
    )
    return jax.shard_map(
        per_device,
        mesh=mesh,
        in_specs=placed,
        out_specs=(P("grp", None, "slab", None, None), P("slab", "grp", None)),
        check_vma=False,
    )
```

```python
import math

import jax
import jax.numpy as jnp
from jax import lax
from jax.experimental import pallas as pl
from jax.experimental.pallas import tpu as pltpu
from jax.sharding import PartitionSpec as P

STEPS = 4
COURANT = 0.5
AMPLITUDE = 4.0
MESH = pl.DeviceIdType.MESH
ROWS = 32
PAD = 8
GROUPS = 32
OWN = 32
INNER = 24
EDGE = 8
LINE = 8
COLUMNS = 4
DIRECT = 128
PIECE = 64


def evolve_kernel(
    pos_hbm, wave_hbm, ids_hbm, mat_hbm, eps_hbm, dens_ref, fwd_ref, adj_ref, out_ref, grad_ref,
    st, coef_ref, tot_ref, pin, eu, pout, sdn, rel, drv, gath, mine, column, line, edge, edge_in, wmat, wtr, base,
    pos_ref, wave_ref, ids_ref, mat_ref, eps_ref,
    small_sem, load_sem, store_sem, own_sem, u1_s, u1_r, u2_s, u2_r, d1_s, d1_r, d2_s, d2_r, rl_s, rl_r,
    gl_s, gl_r, gc_s, gc_r, sc_s, sc_r, sl_s, sl_r, se_s, se_r,
):
    depth, width_x, width_y = coef_ref.shape
    top = depth - 1
    grp, slab = lax.axis_index("grp"), lax.axis_index("slab")
    slabs = lax.axis_size("slab")
    last = slabs - 1
    low, high = slabs // 2 - 1, slabs // 2
    has_up, has_dn = slab < last, slab > 0
    run, col_x, core = grp // LINE, lax.rem(grp // 2, COLUMNS), lax.rem(grp, 2)
    place = run * 2 + core
    middle_run = (run == 1) | (run == 2)
    far_low, far_high = slab == low, slab == high
    relay_up, relay_dn = slab == 0, slab == last
    via_low, via_high = (far_low & middle_run, far_low), (far_high & middle_run, far_high)
    up_relays, dn_relays = (relay_up & middle_run, relay_up), (relay_dn & middle_run, relay_dn)
    inner = pl.ds(PAD, width_x)
    near = pl.ds(0, DIRECT)
    fars = [pl.ds(DIRECT + p * PIECE, PIECE) for p in range(2)]
    kept_rows = [pl.ds(p * PIECE, PIECE) for p in range(2)]
    fields = (fwd_ref, adj_ref)

    def copy_to(src, dst, send, recv, to_slab):
        return pltpu.make_async_remote_copy(
            src_ref=src, dst_ref=dst, send_sem=send, recv_sem=recv, device_id=(grp, to_slab), device_id_type=MESH)

    def u1(ev, n):
        return copy_to(pout.at[ev, n, near, :], pin.at[ev, n, near, :], u1_s.at[ev, n], u1_r.at[ev, n], slab + 1)

    def u2(ev, n, p):
        return copy_to(pout.at[ev, n, fars[p], :], pin.at[ev, n, fars[p], :], u2_s.at[ev, n, p], u2_r.at[ev, n, p], slab + 1)

    def u2_via(ev, n, p):
        return copy_to(pout.at[ev, n, fars[p], :], rel.at[ev, n, kept_rows[p], :], u2_s.at[ev, n, p], rl_r.at[ev, n, p], 0)

    def relay_u2(ev, n, p):
        return copy_to(rel.at[ev, n, kept_rows[p], :], pin.at[ev, n, fars[p], :], rl_s.at[ev, n, p], u2_r.at[ev, n, p], high)

    def d1(ev, n, src):
        return copy_to(src, eu.at[ev, n, near, :], d1_s.at[ev, n], d1_r.at[ev, n], slab - 1)

    def d2(ev, n, p, src):
        return copy_to(src, eu.at[ev, n, fars[p], :], d2_s.at[ev, n, p], d2_r.at[ev, n, p], slab - 1)

    def d2_via(ev, n, p, src):
        return copy_to(src, rel.at[ev, n, kept_rows[p], :], d2_s.at[ev, n, p], rl_r.at[ev, n, p], last)

    def relay_d2(ev, n, p):
        return copy_to(rel.at[ev, n, kept_rows[p], :], eu.at[ev, n, fars[p], :], rl_s.at[ev, n, p], d2_r.at[ev, n, p], low)

    def send_up(ev, n):
        @pl.when(has_up)
        def _():
            for p in (1, 0):

                @pl.when(via_low[p])
                def _():
                    u2_via(ev, n, p).start()

                @pl.when(jnp.logical_not(via_low[p]))
                def _():
                    u2(ev, n, p).start()

            u1(ev, n).start()

    def send_far_dn(ev, n, srcs):
        for p in (1, 0):

            @pl.when(via_high[p])
            def _():
                d2_via(ev, n, p, srcs[p]).start()

            @pl.when(jnp.logical_not(via_high[p]))
            def _():
                d2(ev, n, p, srcs[p]).start()

    def send_dn(ev, n):
        @pl.when(has_dn)
        def _():
            send_far_dn(ev, n, [sdn.at[ev, n - 1, rows, :] for rows in fars])
            d1(ev, n, sdn.at[ev, n - 1, near, :]).start()

    def send_dn_first(ev):
        f = fields[ev]

        @pl.when(has_dn)
        def _():
            send_far_dn(ev, 0, [f.at[0, 1, 0, rows, :] for rows in kept_rows])
            d1(ev, 0, f.at[0, 0, 0]).start()

    def forward(ev, n):
        for p in (1, 0):

            @pl.when(up_relays[p])
            def _():
                u2_via(ev, n, p).wait_recv()
                relay_u2(ev, n, p).start()

            @pl.when(dn_relays[p])
            def _():
                d2_via(ev, n, p, rel.at[ev, n, kept_rows[p], :]).wait_recv()
                relay_d2(ev, n, p).start()

    def peer_copy(src, dst, send, recv, peer):
        return pltpu.make_async_remote_copy(
            src_ref=src, dst_ref=dst, send_sem=send, recv_sem=recv, device_id=(peer, slab), device_id_type=MESH)

    def peer_of(d):
        return lax.rem(grp + d, GROUPS)

    def rows_of(k, count):
        return pl.ds(pl.multiple_of(k * count, 8), count)

    def slot_of(g):
        return lax.rem(g // 2, COLUMNS) * LINE + (g // LINE) * 2 + lax.rem(g, 2)

    def line_peer(q):
        other = lax.rem(place + q, LINE)
        return other, (other // 2) * LINE + col_x * 2 + lax.rem(other, 2)

    def column_peer(p):
        other = lax.rem(col_x + p, COLUMNS)
        return other, run * LINE + other * 2 + core

    def gather_line(q, sender):
        rows = gath.at[rows_of(col_x * LINE + sender, OWN), :]
        return peer_copy(dens_ref, rows, gl_s.at[q], gl_r.at[sender], line_peer(q)[1])

    def gather_column(p, sender, which, src=None):
        rows = gath.at[rows_of(sender * LINE + which, OWN), :]
        return peer_copy(rows if src is None else src, rows, gc_s.at[p, which], gc_r.at[sender, which], column_peer(p)[1])

    def sums_column(p, sender):
        other, peer = column_peer(p)
        return peer_copy(mine.at[rows_of(other, LINE * INNER), :], column.at[rows_of(sender, LINE * INNER), :],
                         sc_s.at[p], sc_r.at[sender], peer)

    def sums_line(q, sender):
        other, peer = line_peer(q)
        kept = rows_of(col_x * LINE + other, INNER)
        return peer_copy(mine.at[kept, :], line.at[rows_of(sender, INNER), :], sl_s.at[q], sl_r.at[sender], peer)

    def sums_edge(d, sender):
        peer = peer_of(d)
        return peer_copy(edge.at[rows_of(slot_of(peer), EDGE), :], edge_in.at[rows_of(slot_of(sender), EDGE), :],
                         se_s, se_r, peer)

    barrier = pltpu.get_barrier_semaphore()

    @pl.loop(1, GROUPS)
    def _(d):
        pl.semaphore_signal(barrier, inc=1, device_id=(peer_of(d), slab), device_id_type=MESH)

    def greet(cond, to_slab):
        @pl.when(cond)
        def _():
            pl.semaphore_signal(barrier, inc=1, device_id=(grp, to_slab), device_id_type=MESH)

    greet(has_up, slab + 1)
    greet(has_dn, slab - 1)
    greet(far_low | far_high, 0)
    greet(far_low | far_high, last)
    greet(relay_up | relay_dn, low)
    greet(relay_up | relay_dn, high)
    smalls = [
        pltpu.make_async_copy(src, dst, small_sem.at[i])
        for i, (src, dst) in enumerate(
            ((pos_hbm, pos_ref), (wave_hbm, wave_ref), (ids_hbm, ids_ref), (mat_hbm, mat_ref), (eps_hbm, eps_ref))
        )
    ]
    for copy in smalls:
        copy.start()
    own_copy = pltpu.make_async_copy(dens_ref, gath.at[rows_of(slot_of(grp), OWN), :], own_sem)
    own_copy.start()
    for ev in range(2):
        pltpu.make_async_copy(fields[ev].at[0], st.at[ev, :, :, inner, :], load_sem.at[ev]).start()

    zeros = jnp.zeros((PAD, width_y), jnp.float32)

    @pl.loop(0, depth)
    def _(z):
        for ev in range(2):
            for c in (1, 2):
                st[ev, c, z, PAD + width_x :, :] = zeros
            for c in (4, 5):
                st[ev, c, z, :PAD, :] = zeros

    for copy in smalls:
        copy.wait()
    row = lax.broadcasted_iota(jnp.int32, (width_x, width_y), 0)
    col = lax.broadcasted_iota(jnp.int32, (width_x, width_y), 1)
    dx = (row - pos_ref[0, 1]).astype(jnp.float32) / (width_x / 4.0)
    dy = (col - pos_ref[0, 2]).astype(jnp.float32) / (width_y / 4.0)
    profile = jnp.exp(-0.5 * (dx * dx + dy * dy))
    wave = jnp.full((8, width_y), wave_ref[0], jnp.int32).astype(jnp.float32)
    omega = 2.0 * math.pi / (6.0 + 2.0 * wave)
    for n in range(STEPS):
        drv[n] = (AMPLITUDE * jnp.sin(omega * (n + 1.0)))[:1] * profile

    blocks = ids_ref.shape[0]
    block_rows = width_x // blocks
    slot = lax.rem(col, blocks)
    target = col // blocks
    for k in range(blocks):
        here = (k // 2 % COLUMNS) * LINE + (k // LINE) * 2 + k % 2
        target = target + jnp.where(slot == here, ids_ref[k] * block_rows, 0)
    apart = jnp.abs(row - target)
    weights = jnp.where(apart == 0, 0.5, jnp.where(apart == 1, 0.25, 0.0))
    wmat[...] = jnp.concatenate([weights, weights], axis=1).astype(jnp.bfloat16)
    wtr[...] = jnp.concatenate([weights.T, weights.T], axis=1).astype(jnp.bfloat16)
    part = lax.broadcasted_iota(jnp.int32, (8, width_y), 0) // block_rows
    per_tile = 8 // block_rows
    for tile in range(width_x // 8):
        value = jnp.zeros((8, width_y), jnp.float32)
        for q in range(per_tile):
            value = jnp.where(part == q, eps_ref[mat_ref[tile * per_tile + q]], value)
        base[8 * tile : 8 * tile + 8, :] = value
    lane = lax.broadcasted_iota(jnp.int32, (ROWS, width_y), 1)
    is_first, is_last = lane == 0, lane == width_y - 1

    @pl.when(jnp.logical_not(has_up))
    def _():
        eu[...] = jnp.zeros_like(eu)

    @pl.when(jnp.logical_not(has_dn))
    def _():
        pin[...] = jnp.zeros_like(pin)

    def next_y(v):
        return jnp.where(is_last, 0.0, pltpu.roll(v, width_y - 1, axis=1))

    def prev_y(v):
        return jnp.where(is_first, 0.0, pltpu.roll(v, 1, axis=1))

    def chunks():
        return [(r, pl.ds(PAD + r, ROWS)) for r in range(0, width_x, ROWS)]

    def h_layer(ev, z, above):
        for r, here in chunks():
            ahead = pl.ds(PAD + r + 1, ROWS)
            ex, ey, ez = (st[ev, c, z, here, :] for c in range(3))
            exu, eyu = above(r)
            dyz = next_y(ez) - ez
            dyx = next_y(ex) - ex
            st[ev, 3, z, here, :] += -COURANT * (dyz - (eyu - ey))
            st[ev, 4, z, here, :] += -COURANT * ((exu - ex) - (st[ev, 2, z, ahead, :] - ez))
            st[ev, 5, z, here, :] += -COURANT * ((st[ev, 1, z, ahead, :] - ey) - dyx)

    def top_part(ev, n):
        for r, here in chunks():
            ahead = pl.ds(PAD + r + 1, ROWS)
            ex, ey, ez = (st[ev, c, top, here, :] for c in range(3))
            out = pl.ds(r, ROWS)
            pout[ev, n, pl.ds(0 * width_x + r, ROWS), :] = st[ev, 3, top, here, :] - COURANT * ((next_y(ez) - ez) + ey)
            pout[ev, n, pl.ds(1 * width_x + r, ROWS), :] = st[ev, 4, top, here, :] + COURANT * ((st[ev, 2, top, ahead, :] - ez) + ex)

    def h_top(ev, n):
        for r, here in chunks():
            ahead = pl.ds(PAD + r + 1, ROWS)
            out = pl.ds(r, ROWS)
            ex, ey = (st[ev, c, top, here, :] for c in range(2))
            st[ev, 3, top, here, :] = pout[ev, n, pl.ds(0 * width_x + r, ROWS), :] + COURANT * eu[ev, n, pl.ds(1 * width_x + r, ROWS), :]
            st[ev, 4, top, here, :] = pout[ev, n, pl.ds(1 * width_x + r, ROWS), :] - COURANT * eu[ev, n, pl.ds(0 * width_x + r, ROWS), :]
            st[ev, 5, top, here, :] += -COURANT * ((st[ev, 1, top, ahead, :] - ey) - (next_y(ex) - ex))

    for ev in range(2):
        pltpu.make_async_copy(fields[ev].at[0], st.at[ev, :, :, inner, :], load_sem.at[ev]).wait()
        top_part(ev, 0)
    extra = jnp.where(far_low | far_high | relay_up | relay_dn, 2, 0)
    pl.semaphore_wait(barrier, GROUPS - 1 + has_up.astype(jnp.int32) + has_dn.astype(jnp.int32) + extra)

    @pl.loop(1, LINE)
    def _(q):
        gather_line(q, place).start()

    @pl.loop(1, COLUMNS)
    def _(p):
        gather_column(p, col_x, place, dens_ref).start()

    send_dn_first(0)
    send_up(0, 0)

    def e_layer(ev, n, z, below, send=None):
        plane = jnp.where((slab * depth + z == pos_ref[0, 0]) & (ev == 0), 1.0, 0.0)
        for r, here in chunks():
            back = pl.ds(PAD + r - 1, ROWS)
            out = pl.ds(r, ROWS)
            hx, hy, hz = (st[ev, c, z, here, :] for c in range(3, 6))
            hxd, hyd = below(r)
            coef = coef_ref[z, out, :]
            ex = st[ev, 0, z, here, :] + coef * ((hz - prev_y(hz)) - (hy - hyd))
            ey = st[ev, 1, z, here, :] + coef * ((hx - hxd) - (hz - st[ev, 5, z, back, :]))
            ez = st[ev, 2, z, here, :] + coef * ((hy - st[ev, 4, z, back, :]) - (hx - prev_y(hx)))
            ez = ez + plane * drv[n, out, :]
            for c, v in enumerate((ex, ey, ez)):
                st[ev, c, z, here, :] = v
            if send is not None:
                for c in range(2):
                    send[pl.ds(c * width_x + r, ROWS), :] = (ex, ey, ez)[c]

    def filter_y(v):
        left = jnp.where(col == 0, 0.0, pltpu.roll(v, 1, axis=1))
        right = jnp.where(col == width_y - 1, 0.0, pltpu.roll(v, width_y - 1, axis=1))
        return (left + 2.0 * v + right) * 0.25

    def mixed(w, v):
        head = v.astype(jnp.bfloat16)
        rest = (v - head.astype(jnp.float32)).astype(jnp.bfloat16)
        return jnp.dot(w[...], jnp.concatenate([head, rest], axis=0), preferred_element_type=jnp.float32)

    def h_inside(ev, z):
        h_layer(ev, z, lambda r: (st[ev, 0, z + 1, pl.ds(PAD + r, ROWS), :], st[ev, 1, z + 1, pl.ds(PAD + r, ROWS), :]))

    def below(ev, z):
        return lambda r: (st[ev, 3, z - 1, pl.ds(PAD + r, ROWS), :], st[ev, 4, z - 1, pl.ds(PAD + r, ROWS), :])

    def add_total(n, z):
        for r, here in chunks():
            out = pl.ds(r, ROWS)
            new = sum(st[0, c, z, here, :] * st[1, c, z, here, :] for c in range(3))
            tot_ref[z, out, :] = jnp.where(n == 0, 0.0, tot_ref[z, out, :]) + new

    def gather():
        own_copy.wait()

        @pl.loop(1, LINE)
        def _(q):
            which = line_peer(q)[0]
            gather_line(q, which).wait_recv()

            @pl.loop(1, COLUMNS)
            def _(p):
                gather_column(p, col_x, which).start()

        send_dn_first(1)
        send_up(1, 0)
        forward(0, 0)
        forward(1, 0)

        @pl.loop(0, LINE)
        def _(which):
            @pl.loop(1, COLUMNS)
            def _(p):
                gather_column(p, column_peer(p)[0], which).wait_recv()

    def make_coef(z):
        rows = jnp.concatenate(
            [gath[pl.ds(z * block_rows + j, blocks, stride=OWN), :] for j in range(block_rows)], axis=0
        )
        coef_ref[z] = 0.5 / (base[...] + 3.0 * mixed(wmat, filter_y(rows)))

    scale = 3.0 / (STEPS * math.sqrt(GROUPS))

    def pack_sums(z, packed, first, count):
        back = mixed(wtr, filter_y(tot_ref[z])) * scale
        for j in range(block_rows):
            packed[pl.ds(first + j, blocks, stride=count), :] = back[j * blocks : (j + 1) * blocks]

    half = jnp.where(has_dn, COURANT, 0.0)

    def below_first(ev, n):
        def values(r):
            out, here = pl.ds(r, ROWS), pl.ds(PAD + r, ROWS)
            return (pin[ev, n, pl.ds(0 * width_x + r, ROWS), :] + half * st[ev, 1, 0, here, :], pin[ev, n, pl.ds(1 * width_x + r, ROWS), :] - half * st[ev, 0, 0, here, :])

        return values

    def edges(ev, n, sending):
        @pl.when(has_up)
        def _():
            d1(ev, n, sdn.at[ev, n, near, :]).wait_recv()
            for p in range(2):
                d2(ev, n, p, sdn.at[ev, n, fars[p], :]).wait_recv()

        h_top(ev, n)
        e_layer(ev, n, top, below(ev, top))
        if sending:
            top_part(ev, n + 1)
            send_up(ev, n + 1)

        @pl.when(has_dn)
        def _():
            u1(ev, n).wait_recv()
            for p in range(2):
                u2(ev, n, p).wait_recv()

        e_layer(ev, n, 0, below_first(ev, n), sdn.at[ev, n])
        if sending:
            send_dn(ev, n + 1)

    def h_rest(ev):
        h_inside(ev, 0)

        @pl.loop(1, top, step=2)
        def _(z):
            h_inside(ev, z)
            h_inside(ev, z + 1)

    def e_rest(ev, n):
        @pl.loop(1, top, step=2)
        def _(z):
            e_layer(ev, n, z, below(ev, z))
            e_layer(ev, n, z + 1, below(ev, z + 1))

    @pl.loop(0, 2 * STEPS - 2)
    def _(i):
        n, ev = i // 2, lax.rem(i, 2)
        h_rest(ev)

        @pl.when(i == 0)
        def _():
            gather()
            make_coef(0)
            make_coef(top)

        edges(ev, n, True)

        @pl.when(i == 0)
        def _():
            @pl.loop(1, top)
            def _(z):
                make_coef(z)

        e_rest(ev, n)

        @pl.when((i > 0) & (i < 2 * STEPS - 3))
        def _():
            forward(1 - ev, (i + 1) // 2)

        @pl.when(ev == 1)
        def _():
            @pl.loop(0, depth)
            def _(z):
                add_total(n, z)

    def settle():
        @pl.loop(1, LINE)
        def _(q):
            gather_line(q, place).wait_send()

        @pl.loop(1, COLUMNS)
        def _(p):
            sums_column(p, col_x).wait_send()

            @pl.loop(0, LINE)
            def _(which):
                gather_column(p, col_x, which).wait_send()

        @pl.loop(0, 2 * STEPS)
        def _(i):
            n, ev = i // 2, lax.rem(i, 2)

            @pl.when(has_up)
            def _():
                u1(ev, n).wait_send()
                for p in range(2):
                    u2(ev, n, p).wait_send()

            @pl.when(has_dn)
            def _():
                d1(ev, n, sdn.at[ev, n, near, :]).wait_send()
                for p in range(2):
                    d2(ev, n, p, sdn.at[ev, n, fars[p], :]).wait_send()

            for p in range(2):

                @pl.when(up_relays[p])
                def _():
                    relay_u2(ev, n, p).wait_send()

                @pl.when(dn_relays[p])
                def _():
                    relay_d2(ev, n, p).wait_send()

    n = STEPS - 1

    @pl.loop(0, 2)
    def _(ev):
        h_rest(ev)
        e_rest(ev, n)

        @pl.when(ev == 0)
        def _():
            forward(0, n)

    @pl.loop(1, top)
    def _(z):
        add_total(n, z)
        pack_sums(z, mine, (z - 1) * block_rows, INNER)

    @pl.loop(1, COLUMNS)
    def _(p):
        sums_column(p, col_x).start()

    forward(1, n)

    @pl.loop(0, 2)
    def _(ev):
        edges(ev, n, False)

        @pl.when(ev == 0)
        def _():
            pltpu.make_async_copy(st.at[0, :, :, inner, :], out_ref.at[0], store_sem).start()

    add_total(n, 0)
    add_total(n, top)
    pack_sums(0, edge, 0, EDGE)
    pack_sums(top, edge, block_rows, EDGE)

    @pl.loop(1, GROUPS)
    def _(d):
        sums_edge(d, grp).start()

    @pl.loop(1, COLUMNS)
    def _(p):
        sender = column_peer(p)[0]
        sums_column(p, sender).wait_recv()
        kept = rows_of(col_x, LINE * INNER)
        mine[kept, :] += column[rows_of(sender, LINE * INNER), :]

    @pl.loop(1, LINE)
    def _(q):
        sums_line(q, place).start()

    settle()

    def add_line(q, acc):
        sender = line_peer(q)[0]
        sums_line(q, sender).wait_recv()
        return acc + line[rows_of(sender, INNER), :]

    middle = lax.fori_loop(1, LINE, add_line, mine[rows_of(slot_of(grp), INNER), :])
    for z in range(1, top):
        grad_ref[z * block_rows : (z + 1) * block_rows, :] = middle[(z - 1) * block_rows : z * block_rows]

    others = pl.ds(0, (GROUPS - 1) * EDGE)
    all_edges = peer_copy(edge.at[others, :], edge_in.at[others, :], se_s, se_r, peer_of(1))
    edge_in[rows_of(slot_of(grp), EDGE), :] = edge[rows_of(slot_of(grp), EDGE), :]
    all_edges.wait_recv()
    ends = edge_in[0:EDGE, :]
    for other in range(1, GROUPS):
        ends = ends + edge_in[other * EDGE : (other + 1) * EDGE, :]
    grad_ref[0:block_rows, :] = ends[:block_rows]
    grad_ref[top * block_rows : depth * block_rows, :] = ends[block_rows:]

    pltpu.make_async_copy(st.at[0, :, :, inner, :], out_ref.at[0], store_sem).wait()

    @pl.loop(1, LINE)
    def _(q):
        sums_line(q, place).wait_send()

    all_edges.wait_send()


def per_device(
    fwd_fields, adj_fields, density, block_ids, material_idx, material_eps, source_pos, wave_idx
):
    depth, width_x, width_y = fwd_fields.shape[2:]
    f32 = jnp.float32
    layer = (width_x, width_y)
    rows = density.shape[0] * density.shape[1]
    vmem = pl.BlockSpec(memory_space=pltpu.VMEM)
    anywhere = pl.BlockSpec(memory_space=pl.ANY)
    hbm = pl.BlockSpec(memory_space=pltpu.HBM)
    dma = pltpu.SemaphoreType.DMA
    steps, pieces = dma((2, STEPS)), dma((2, STEPS, 2))
    def in_hbm(a):
        return pltpu.with_memory_space_constraint(a, pltpu.HBM)

    finals, grad = pl.pallas_call(
        evolve_kernel,
        out_shape=(jax.ShapeDtypeStruct(fwd_fields.shape, f32), jax.ShapeDtypeStruct((rows, width_y), f32)),
        in_specs=[hbm] * 8,
        out_specs=(anywhere, vmem),
        scratch_shapes=[
            pltpu.VMEM((2, 6, depth, width_x + 2 * PAD, width_y), f32),
            pltpu.VMEM((depth, *layer), f32),
            pltpu.VMEM((depth, *layer), f32),
            *[pltpu.VMEM((2, STEPS, 2 * width_x, width_y), f32)] * 4,
            pltpu.VMEM((2, STEPS, 2 * width_x - DIRECT, width_y), f32),
            pltpu.VMEM((STEPS, *layer), f32),
            pltpu.VMEM((GROUPS * OWN, width_y), f32),
            pltpu.VMEM((GROUPS * INNER, width_y), f32),
            pltpu.VMEM((GROUPS * INNER, width_y), f32),
            pltpu.VMEM((LINE * INNER, width_y), f32),
            pltpu.VMEM((GROUPS * EDGE, width_y), f32),
            pltpu.VMEM((GROUPS * EDGE, width_y), f32),
            pltpu.VMEM((width_x, 2 * width_x), jnp.bfloat16),
            pltpu.VMEM((width_x, 2 * width_x), jnp.bfloat16),
            pltpu.VMEM(layer, f32),
            *(pltpu.SMEM(a.shape, a.dtype) for a in (source_pos, wave_idx, block_ids, material_idx, material_eps)),
            dma((5,)), dma((2,)), dma(()), dma(()), steps, steps, pieces, pieces, steps, steps, pieces, pieces, pieces, pieces,
            *[dma((LINE,))] * 2, *[dma((COLUMNS, LINE))] * 2, *[dma((COLUMNS,))] * 2, *[dma((LINE,))] * 2, dma(()), dma(()),
        ],
        compiler_params=pltpu.CompilerParams(collective_id=0, has_side_effects=True, vmem_limit_bytes=48 << 20),
        name="evolve",
    )(in_hbm(source_pos), wave_idx, in_hbm(block_ids), in_hbm(material_idx), in_hbm(material_eps), in_hbm(density.reshape(rows, width_y)), fwd_fields, adj_fields)
    return finals, grad.reshape(density.shape)


def solution(mesh):
    placed = (
        P("grp", None, "slab", None, None),
        P("grp", None, "slab", None, None),
        P("slab", "grp", None),
        P(),
        P(),
        P(),
        P("grp", None),
        P("grp"),
    )
    return jax.shard_map(
        per_device,
        mesh=mesh,
        in_specs=placed,
        out_specs=(P("grp", None, "slab", None, None), P("slab", "grp", None)),
        check_vma=False,
    )
```
